512 devices in a mesh: section: 2 (over x_hi), dp: 8 (over y, core), tensor: 32 (over x_lo, z).
Axes of the slice: x: 4 (x_hi: 2, x_lo: 2; x = x_hi * 2 + x_lo), y: 4, z: 16, core: 2. Of those that a mesh axis runs over, the one named last changes fastest.
Arguments:
- tokens_in: bfloat16 [2, 7168, 2048], P(None, 'tensor', 'dp'), may hold values from -47 to 47
- section_proj: bfloat16 [2, 7168, 7168], P('section', 'tensor'), may hold values from -0.0625 to 0.0625
- section_gain: bfloat16 [2, 7168], P('section', 'tensor'), may hold values from 0.099609375 to 1.8984375
- final_gain: bfloat16 [7168], P('tensor'), may hold values from 0.099609375 to 1.8984375
- score_weight: bfloat16 [7168], P('tensor'), may hold values from -0.0625 to 0.0625
- labels: int32 [2, 2048], P(None, 'dp'), may hold values from 0 to 2
- loss_mask: int32 [2, 2048], P(None, 'dp'), may hold values 0 or 1
- segment_ids: int32 [2, 2048], P(None, 'dp'), may hold values from 0 to 15, never falling along the last dimension, each value on 1 to 512 neighbouring positions
Outputs:
- section_out: bfloat16 [2, 2, 7168, 2048], P('section', None, 'tensor', 'dp')
- segment_loss: float32 [2, 16], replicated
The draws below stay inside these ranges and needn't reach their ends.
Inputs may be any that keep to these rules, and one draw needn't show every extreme that they name: `segment_ids`: within a micro-batch segment numbers never fall along the tokens; each segment has 1 to 512 tokens.
All inputs are finite; a program needn't handle non-finite values. No bound on the sum of `loss_mask` on one device may be relied on, other than what follows from the above.
Results may differ from the reference program's by a relative error of at most 0.0045.
Values may be sent and summed in bfloat16 or wider, within the bound.
No kernel may reach another device: no remote copies, remote signals or barrier semaphores. Data moves between devices by JAX's collectives and lax.ppermute only.
A program may use at most 64 MiB of HBM per device.

```python
import math
import jax
import jax.numpy as jnp
import numpy as np
from jax import lax

D = 7168
TOK_DEV = 256
MB = 2
SEGS = 16
LEVELS = 3
TOKENS = 2048
N_SECTION = 2


def draw_tokens_in(key, part):
    key_base, key_rows, key_cols = jax.random.split(key, 3)
    shape = (MB, D, TOKENS)
    base = jnp.clip(jax.random.normal(key_base, shape, jnp.float32), -5.0, 5.0)
    token_scale = jnp.exp(jax.random.uniform(key_rows, (MB, 1, TOKENS), jnp.float32, math.log(0.3), math.log(3.0)))
    feature_scale = jnp.exp(jax.random.uniform(key_cols, (1, D, 1), jnp.float32, math.log(0.3), math.log(3.0)))
    return (base * token_scale * feature_scale).astype(jnp.bfloat16)


def set_ends(entries, key, smallest, largest):
    index_at = [jax.random.randint(jax.random.fold_in(key, axis), (), 0, length) for axis, length in enumerate(entries.shape)]
    longest = entries.shape.index(max(entries.shape))
    next_to = index_at[:longest] + [(index_at[longest] + 1) % entries.shape[longest]] + index_at[longest + 1:]
    return entries.at[tuple(index_at)].set(smallest).at[tuple(next_to)].set(largest)


def shard_levels(rng, dims, cuts, low, top_value):
    loudness = 1.0
    for axis_at, parts in cuts:
        heights = jax.random.uniform(jax.random.fold_in(jax.random.fold_in(rng, 6), axis_at), (parts,), jnp.float32, low / len(cuts), top_value / len(cuts))
        loudness = loudness * jnp.repeat(jnp.exp(heights), dims[axis_at] // parts).reshape((-1,) + (1,) * (len(dims) - 1 - axis_at))
    return loudness


def split_up(amount, total, limit, skew):
    weights = [(1 << 20) // math.isqrt(standing ** skew) + 1 for standing in range(2, amount + 1)]
    surplus, counts = total - limit - (amount - 1), [1] * (amount - 1)
    while surplus > 0:
        candidates = [i for i in range(amount - 1) if counts[i] < limit]
        whole, budget = sum([weights[i] for i in candidates]), surplus
        for i in candidates:
            more = min(limit - counts[i], max(1, budget * weights[i] // whole), surplus)
            counts[i] = counts[i] + more
            surplus = surplus - more
    return np.array([limit] + counts)


def ragged_sizes(rng, count, total, most, slope):
    if count == 2:
        one = jax.random.randint(rng, (), max(1, total - most), min(most, total - 1) + 1)
        return jnp.stack([one, total - one])
    tallies = jnp.asarray(split_up(count, total, most, slope), jnp.int32)
    couples = (count - 1) // 2
    source_of, sink = tallies[1:1 + 2 * couples:2], tallies[2:2 + 2 * couples:2]
    margin = jnp.minimum(source_of - 1, most - sink)
    moved = jax.random.randint(jax.random.fold_in(rng, 1), (couples,), 0, 1 << 20) % (margin + 1)
    tallies = tallies.at[1:1 + 2 * couples:2].set(source_of - moved).at[2:2 + 2 * couples:2].set(sink + moved)
    return tallies[jax.random.permutation(jax.random.fold_in(rng, 2), count)]


def gaussian(key, extent, width, bound, pieces=(), kind=jnp.bfloat16):
    entries = width * jax.random.normal(key, extent, jnp.float32)
    if pieces:
        entries = entries * shard_levels(key, extent, pieces, -0.22, 0.18)
    return jnp.clip(entries, -bound, bound).astype(kind)


def setup_inputs(seed: int = 0) -> dict:
    splits = jax.random.split(jax.random.key(seed), 9)
    tokens_in = draw_tokens_in(jax.random.fold_in(splits[8], 71), 0)
    section_proj = gaussian(splits[1], (N_SECTION, D, D), D ** -0.5, 0.0625, ((0, 2), (1, 32)))
    section_gain = jnp.clip(1.0 + 0.18 * jax.random.normal(splits[2], (N_SECTION, D), jnp.float32), 0.099609375, 1.8984375).astype(jnp.bfloat16)
    final_gain = jnp.clip(1.0 + 0.18 * jax.random.normal(splits[3], (D,), jnp.float32), 0.099609375, 1.8984375).astype(jnp.bfloat16)
    score_weight = gaussian(splits[4], (D,), D ** -0.5, 0.0625, ((0, 32),))
    labels = set_ends(jax.random.randint(splits[5], (MB, TOKENS), 0, LEVELS), jax.random.fold_in(splits[5], 1), 0, LEVELS - 1).astype(jnp.int32)
    loss_mask = set_ends((jax.random.randint(splits[6], (MB, TOKENS), 0, 2) < 1).astype(jnp.int32), jax.random.fold_in(splits[6], 1), 0, 1)
    segment_ids = jax.vmap(lambda own: jnp.searchsorted(jnp.cumsum(ragged_sizes(own, SEGS, TOKENS, 2 * TOK_DEV, 2)), jnp.arange(TOKENS), side="right"))(jax.random.split(splits[7], MB)).reshape((MB, TOKENS)).astype(jnp.int32)
    return dict(tokens_in=tokens_in, section_proj=section_proj, section_gain=section_gain, final_gain=final_gain, score_weight=score_weight, labels=labels, loss_mask=loss_mask, segment_ids=segment_ids)


epsilon = 1e-05

def apply_block(rows_in, weight, gain):
    as_float = rows_in.astype(jnp.float32)
    inv_root = lax.rsqrt(lax.optimization_barrier(jnp.mean(as_float * as_float, axis=-1, keepdims=True)) + epsilon)
    normed = (as_float * inv_root * gain.astype(jnp.float32)).astype(jnp.bfloat16)
    mixed = jnp.dot(normed, weight.T, preferred_element_type=jnp.float32)
    return (as_float + jax.nn.silu(mixed)).astype(jnp.bfloat16)

def reference(tokens_in, section_proj, section_gain, final_gain, score_weight, labels, loss_mask, segment_ids):
    first_rows = []
    second_rows = []
    loss_rows = []
    segment_range = jnp.arange(SEGS, dtype=jnp.int32)
    head_vector = final_gain.astype(jnp.float32) * score_weight.astype(jnp.float32)
    for micro in range(MB):
        after_first = apply_block(tokens_in[micro].T, section_proj[0], section_gain[0])
        after_second = apply_block(after_first, section_proj[1], section_gain[1])
        first_rows.append(after_first.T)
        second_rows.append(after_second.T)
        as_float = after_second.astype(jnp.float32)
        inv_root = lax.rsqrt(lax.optimization_barrier(jnp.mean(as_float * as_float, axis=-1)) + epsilon)
        scores = lax.optimization_barrier(jnp.sum(as_float * head_vector[None, :], axis=-1)) * inv_root
        target = labels[micro].astype(jnp.float32) - 1.0
        weight_mask = loss_mask[micro].astype(jnp.float32)
        offset_err = scores - target
        squared = weight_mask * offset_err * offset_err
        member = (segment_ids[micro][:, None] == segment_range[None, :]).astype(jnp.float32)
        loss_sums = jnp.dot(squared, member, precision=lax.Precision.HIGHEST)
        counted = jnp.dot(weight_mask, member, precision=lax.Precision.HIGHEST)
        loss_rows.append(loss_sums / jnp.maximum(counted, 1.0))
    section_out = jnp.stack([jnp.stack(first_rows), jnp.stack(second_rows)])
    return (section_out, jnp.stack(loss_rows))
```

```python
import jax
import jax.numpy as jnp
from jax import lax
from jax.experimental import pallas as pl
from jax.experimental.pallas import tpu as pltpu
from jax.sharding import Mesh
from jax.sharding import PartitionSpec as P

D = 7168
SEGS = 16
EPS = 1e-05
F = 224
T = 256
KH = D // 2
R = 240
HALF = F // 2
F32 = jnp.float32
BF16 = jnp.bfloat16
Z = ("h", "p")
VMEM_LIMIT = 40 * 1024 * 1024


def vmem():
    return pl.BlockSpec(memory_space=pltpu.VMEM)


def smem():
    return pl.BlockSpec(memory_space=pltpu.SMEM)


def anywhere():
    return pl.BlockSpec(memory_space=pl.ANY)


def pack_block(rows, gain, block_ref):
    block_ref[0:F, :] = (rows * gain).astype(BF16)
    squares = jnp.sum(rows * rows, axis=0, keepdims=True)
    first = squares.astype(BF16)
    rest = squares - first.astype(F32)
    second = rest.astype(BF16)
    third = (rest - second.astype(F32)).astype(BF16)
    at = lax.broadcasted_iota(jnp.int32, (R - F, T), 0)
    tail = jnp.where(at == 0, first.astype(F32), 0.0)
    tail = jnp.where(at == 1, second.astype(F32), tail)
    tail = jnp.where(at == 2, third.astype(F32), tail)
    block_ref[F:R, :] = tail.astype(BF16)


def pack_kernel(rows_ref, gain_ref, block_ref):
    pack_block(rows_ref[...].astype(F32), gain_ref[...].astype(F32), block_ref)


def pack(rows, gain):
    return pl.pallas_call(
        pack_kernel,
        out_shape=jax.ShapeDtypeStruct((R, T), BF16),
        in_specs=[vmem(), vmem()],
        out_specs=vmem(),
        name="pack",
    )(rows, gain)


def product_kernel(
    local_block, at_ref, same_ref, below_ref, above_ref, weight_ref, side_ref, side2_ref,
    over_ref, over2_ref, cross_ref, cross2_ref, own_ref, send_ref, held, values, sems,
):
    section, x, core, parity = at_ref[0], at_ref[1], at_ref[2], at_ref[3]
    columns = pl.ds(pl.multiple_of(x * KH, 128), KH)
    mine = pl.ds(pl.multiple_of(core * HALF, 16), HALF)
    theirs = pl.ds(pl.multiple_of((1 - core) * HALF, 16), HALF)
    far = pl.ds(pl.multiple_of(F + core * HALF, 16), HALF)
    far2 = pl.ds(pl.multiple_of(F + (1 - core) * HALF, 16), HALF)

    def near_copies():
        return [
            pltpu.make_async_copy(weight_ref.at[:, columns], held.at[0:F, :], sems.at[0]),
            pltpu.make_async_copy(side_ref, held.at[far, :], sems.at[1]),
            pltpu.make_async_copy(side2_ref, held.at[far2, :], sems.at[2]),
        ]

    def away_copies():
        return [
            pltpu.make_async_copy(over_ref, held.at[mine, :], sems.at[0]),
            pltpu.make_async_copy(over2_ref, held.at[theirs, :], sems.at[1]),
            pltpu.make_async_copy(cross_ref, held.at[far, :], sems.at[2]),
            pltpu.make_async_copy(cross2_ref, held.at[far2, :], sems.at[3]),
        ]

    @pl.when(section == local_block)
    def _():
        for copy in near_copies():
            copy.start()

    @pl.when(section != local_block)
    def _():
        for copy in away_copies():
            copy.start()

    squares = jnp.zeros((1, T), F32)
    for i in range(8):
        got = same_ref[i]
        here = pl.ds(pl.multiple_of((2 * i + parity) * F, 16), F)
        values[here, :] = got[0:F]
        squares += jnp.sum(got[F:R].astype(F32), axis=0, keepdims=True)
        other = below_ref[i] if i < 4 else above_ref[i - 4]
        there = pl.ds(pl.multiple_of((2 * i + 1 - parity) * F, 16), F)
        values[there, :] = other[0:F]
        squares += jnp.sum(other[F:R].astype(F32), axis=0, keepdims=True)

    @pl.when(section == local_block)
    def _():
        for copy in near_copies():
            copy.wait()

    @pl.when(section != local_block)
    def _():
        for copy in away_copies():
            copy.wait()

    product = jnp.dot(held[...], values[...], preferred_element_type=F32)
    rows = jnp.broadcast_to(squares, (8, T))
    own_ref[0:F, :] = product[0:F]
    own_ref[F:F + 8, :] = rows
    send_ref[0:F, :] = product[F:2 * F]
    send_ref[F:F + 8, :] = rows


def product(local_block, at, same, below, above, weight, received):
    import functools
    out = jax.ShapeDtypeStruct((F + 8, T), F32)
    return pl.pallas_call(
        functools.partial(product_kernel, local_block),
        out_shape=(out, out),
        in_specs=[smem(), vmem(), vmem(), vmem()] + [anywhere()] * 7,
        out_specs=(vmem(), vmem()),
        scratch_shapes=[
            pltpu.VMEM((2 * F, KH), BF16),
            pltpu.VMEM((KH, T), BF16),
            pltpu.SemaphoreType.DMA((4,)),
        ],
        compiler_params=pltpu.CompilerParams(vmem_limit_bytes=VMEM_LIMIT),
        name="product",
    )(at, same, below, above, weight, *received)


def block_rows(own_ref, other_ref, rows_ref):
    squares = own_ref[F:F + 1, :] + other_ref[F:F + 1, :]
    inv_root = lax.rsqrt(squares / D + EPS)
    mixed = (own_ref[0:F, :] + other_ref[0:F, :]) * inv_root
    gated = mixed / (1.0 + jnp.exp(-mixed))
    return (rows_ref[...].astype(F32) + gated).astype(BF16)


def middle_kernel(own_ref, other_ref, rows_ref, gain_ref, out_ref, block_ref):
    out = block_rows(own_ref, other_ref, rows_ref)
    out_ref[...] = out
    pack_block(out.astype(F32), gain_ref[...].astype(F32), block_ref)


def middle(own, other, rows, gain):
    return pl.pallas_call(
        middle_kernel,
        out_shape=(jax.ShapeDtypeStruct((F, T), BF16), jax.ShapeDtypeStruct((R, T), BF16)),
        in_specs=[vmem()] * 4,
        out_specs=(vmem(), vmem()),
        name="middle",
    )(own, other, rows, gain)


def last_kernel(at_ref, own_ref, other_ref, rows_ref, head_ref, out_ref, swap_ref, stats_ref):
    out = block_rows(own_ref, other_ref, rows_ref)
    out_ref[...] = out
    @pl.when(at_ref[0] == 0)
    def _():
        swap_ref[...] = out

    @pl.when(at_ref[0] != 0)
    def _():
        swap_ref[...] = rows_ref[...]

    as_float = out.astype(F32)
    head = head_ref[...]
    squares = jnp.sum(as_float * as_float, axis=0, keepdims=True)
    scores = jnp.sum(as_float * head, axis=0, keepdims=True)
    stats = jnp.concatenate([squares, scores], axis=0)
    for i in range(32):
        stats_ref[i] = stats


def last(at, own, other, rows, head):
    out = jax.ShapeDtypeStruct((F, T), BF16)
    return pl.pallas_call(
        last_kernel,
        out_shape=(out, out, jax.ShapeDtypeStruct((32, 2, T), F32)),
        in_specs=[smem()] + [vmem()] * 4,
        out_specs=(vmem(), vmem(), vmem()),
        name="last",
    )(at, own, other, rows, head)


def loss_kernel(stats_ref, label_ref, mask_ref, segment_ref, sums_ref):
    total = jnp.sum(stats_ref[...], axis=0)
    inv_root = lax.rsqrt(total[0:1] / D + EPS)
    score = total[1:2] * inv_root
    target = label_ref[...].astype(F32) - 1.0
    mask = mask_ref[...].astype(F32)
    err = score - target
    squared = mask * err * err
    member = segment_ref[...] == lax.broadcasted_iota(jnp.int32, (SEGS, T), 0)
    sums = jnp.sum(jnp.where(member, squared, 0.0), axis=1, keepdims=True)
    counts = jnp.sum(jnp.where(member, mask, 0.0), axis=1, keepdims=True)
    lane = lax.broadcasted_iota(jnp.int32, (SEGS, 128), 1)
    sums_ref[...] = jnp.where(lane == 0, sums, jnp.where(lane == 1, counts, 0.0))


def loss_parts(stats, label, mask, segment):
    return pl.pallas_call(
        loss_kernel,
        out_shape=jax.ShapeDtypeStruct((SEGS, 128), F32),
        in_specs=[vmem()] * 4,
        out_specs=vmem(),
        name="loss_parts",
    )(stats, label, mask, segment)


def swapped(value, *axes):
    count = 2 ** len(axes)
    name = axes if len(axes) > 1 else axes[0]
    return lax.ppermute(value, name, [(i, i ^ (count - 1)) for i in range(count)])


def shifted(value, by):
    return lax.ppermute(value, Z, [(i, (i + by) % 16) for i in range(16)])


def gathered(block):
    same = lax.all_gather(block, "h", axis=0, tiled=False)
    return same, shifted(same[0:4], 1), shifted(same[4:8], -1)


def body(
    tokens_in, section_proj, section_gain, final_gain, score_weight, labels, loss_mask, segment_ids
):
    section = lax.axis_index("s")
    x = lax.axis_index("x")
    core = lax.axis_index("c")
    at = jnp.stack([section, x, core, lax.axis_index("p")]).astype(jnp.int32)
    weight = section_proj[0]

    gain = section_gain[0][:, None]
    gain_away = swapped(gain, "s")
    gain0 = jnp.where(section == 0, gain, gain_away)
    gain1 = jnp.where(section == 0, gain_away, gain)

    half = lax.dynamic_slice(weight, (core * HALF, 0), (HALF, D))
    near = lax.dynamic_slice(half, (0, x * KH), (HALF, KH))
    far = lax.dynamic_slice(half, (0, (1 - x) * KH), (HALF, KH))
    side = swapped(far, "x")
    over = swapped(near, "s")
    cross = swapped(far, "s", "x")

    rows = lax.dynamic_index_in_dim(tokens_in, section, 0, keepdims=False)
    same, below, above = gathered(pack(rows, gain0))

    side, over, cross, same = lax.optimization_barrier((side, over, cross, same))
    received = (
        side, swapped(side, "c"), over, swapped(over, "c"), cross, swapped(cross, "c")
    )
    own, send = product(0, at, same, below, above, weight, received)
    first, block = middle(own, swapped(send, "x"), rows, gain1)

    same, below, above = gathered(block)
    own, send = product(1, at, same, below, above, weight, received)
    head = (final_gain.astype(F32) * score_weight.astype(F32))[:, None]
    second, handed, stats = last(at, own, swapped(send, "x"), first, head)
    handed = swapped(handed, "s")

    stats = lax.all_to_all(stats, ("x", "h", "p"), 0, 0, tiled=True)
    pick = lambda value: lax.dynamic_slice(value, (section, 0), (1, T))
    parts = loss_parts(stats, pick(labels), pick(loss_mask), pick(segment_ids))
    parts = jnp.broadcast_to(parts[None, :, 0:2], (16, SEGS, 2))
    parts = lax.all_to_all(parts, ("s", "y", "c"), 0, 0, tiled=True)
    parts = jnp.sum(parts.reshape(2, 8, SEGS, 2), axis=1)
    segment_loss = parts[..., 0] / jnp.maximum(parts[..., 1], 1.0)

    section_out = jnp.where(section == 0, jnp.stack([first, handed]), jnp.stack([handed, second]))
    return section_out[None], segment_loss


def solution(mesh):
    finer = Mesh(mesh.devices.reshape(2, 4, 2, 2, 8, 2), ("s", "y", "c", "x", "h", "p"))
    tensor = ("x", "h", "p")
    dp = ("y", "c")
    in_specs = (
        P(None, tensor, dp),
        P("s", tensor, None),
        P("s", tensor),
        P(tensor),
        P(tensor),
        P(None, dp),
        P(None, dp),
        P(None, dp),
    )
    out_specs = (P("s", None, tensor, dp), P())
    return jax.shard_map(body, mesh=finer, in_specs=in_specs, out_specs=out_specs, check_vma=False)
```

```python
import functools

import jax
import jax.numpy as jnp
from jax import lax
from jax.experimental import pallas as pl
from jax.experimental.pallas import tpu as pltpu
from jax.sharding import Mesh
from jax.sharding import PartitionSpec as P

D = 7168
SEGS = 16
EPS = 1e-05
F = 224
T = 256
KH = D // 2
R = 240
F32 = jnp.float32
BF16 = jnp.bfloat16
Z = ("h", "p")
SMALL = pltpu.CompilerParams(vmem_limit_bytes=4 * 1024 * 1024)
LARGE = pltpu.CompilerParams(vmem_limit_bytes=16 * 1024 * 1024)


def vmem():
    return pl.BlockSpec(memory_space=pltpu.VMEM)


def smem():
    return pl.BlockSpec(memory_space=pltpu.SMEM)


def anywhere():
    return pl.BlockSpec(memory_space=pl.ANY)


def pack_block(rows, gain, block_ref):
    block_ref[0:F, :] = (rows * gain).astype(BF16)
    squares = jnp.sum(rows * rows, axis=0, keepdims=True)
    first = squares.astype(BF16)
    rest = squares - first.astype(F32)
    second = rest.astype(BF16)
    third = (rest - second.astype(F32)).astype(BF16)
    at = lax.broadcasted_iota(jnp.int32, (R - F, T), 0)
    tail = jnp.where(at == 0, first.astype(F32), 0.0)
    tail = jnp.where(at == 1, second.astype(F32), tail)
    tail = jnp.where(at == 2, third.astype(F32), tail)
    block_ref[F:R, :] = tail.astype(BF16)


def pack_kernel(rows_ref, gain_ref, block_ref):
    pack_block(rows_ref[...].astype(F32), gain_ref[...].astype(F32), block_ref)


def pack(rows, gain):
    return pl.pallas_call(
        pack_kernel,
        out_shape=jax.ShapeDtypeStruct((R, T), BF16),
        in_specs=[vmem(), vmem()],
        out_specs=vmem(),
        compiler_params=SMALL,
        name="pack",
    )(rows, gain)


def split_kernel(at_ref, weight_ref, near_ref, far_ref, sems):
    x = at_ref[1]
    near = pl.ds(pl.multiple_of(x * KH, 128), KH)
    far = pl.ds(pl.multiple_of((1 - x) * KH, 128), KH)
    copies = [
        pltpu.make_async_copy(weight_ref.at[:, near], near_ref, sems.at[0]),
        pltpu.make_async_copy(weight_ref.at[:, far], far_ref, sems.at[1]),
    ]
    for copy in copies:
        copy.start()
    for copy in copies:
        copy.wait()


def split(at, weight):
    out = jax.ShapeDtypeStruct((F, KH), BF16)
    return pl.pallas_call(
        split_kernel,
        out_shape=(out, out),
        in_specs=[smem(), anywhere()],
        out_specs=(anywhere(), anywhere()),
        scratch_shapes=[pltpu.SemaphoreType.DMA((2,))],
        compiler_params=SMALL,
        name="split",
    )(at, weight)


def product_kernel(
    local_block, at_ref, same_ref, below_ref, above_ref, near_ref, side_ref, over_ref, cross_ref,
    own_ref, send_ref, held, values, sems,
):
    local = at_ref[0] == local_block
    parity = at_ref[3]

    def copies(first, second):
        return [
            pltpu.make_async_copy(first, held.at[0:F, :], sems.at[0]),
            pltpu.make_async_copy(second, held.at[F:2 * F, :], sems.at[1]),
        ]

    @pl.when(local)
    def _():
        for copy in copies(near_ref, side_ref):
            copy.start()

    @pl.when(jnp.logical_not(local))
    def _():
        for copy in copies(over_ref, cross_ref):
            copy.start()

    squares = jnp.zeros((1, T), F32)
    for i in range(8):
        got = same_ref[i]
        here = pl.ds(pl.multiple_of((2 * i + parity) * F, 16), F)
        values[here, :] = got[0:F]
        squares += jnp.sum(got[F:R].astype(F32), axis=0, keepdims=True)
        other = below_ref[i] if i < 4 else above_ref[i - 4]
        there = pl.ds(pl.multiple_of((2 * i + 1 - parity) * F, 16), F)
        values[there, :] = other[0:F]
        squares += jnp.sum(other[F:R].astype(F32), axis=0, keepdims=True)

    @pl.when(local)
    def _():
        for copy in copies(near_ref, side_ref):
            copy.wait()

    @pl.when(jnp.logical_not(local))
    def _():
        for copy in copies(over_ref, cross_ref):
            copy.wait()

    product = jnp.dot(held[...], values[...], preferred_element_type=F32)
    rows = jnp.broadcast_to(squares, (8, T))
    own_ref[0:F, :] = product[0:F]
    own_ref[F:F + 8, :] = rows
    send_ref[0:F, :] = product[F:2 * F]
    send_ref[F:F + 8, :] = rows


def product(local_block, at, same, below, above, blocks):
    out = jax.ShapeDtypeStruct((F + 8, T), F32)
    return pl.pallas_call(
        functools.partial(product_kernel, local_block),
        out_shape=(out, out),
        in_specs=[smem(), vmem(), vmem(), vmem()] + [anywhere()] * 4,
        out_specs=(vmem(), vmem()),
        scratch_shapes=[
            pltpu.VMEM((2 * F, KH), BF16),
            pltpu.VMEM((KH, T), BF16),
            pltpu.SemaphoreType.DMA((2,)),
        ],
        compiler_params=LARGE,
        name="product",
    )(at, same, below, above, *blocks)


def block_rows(own_ref, other_ref, rows_ref):
    squares = own_ref[F:F + 1, :] + other_ref[F:F + 1, :]
    inv_root = lax.rsqrt(squares / D + EPS)
    mixed = (own_ref[0:F, :] + other_ref[0:F, :]) * inv_root
    gated = mixed / (1.0 + jnp.exp(-mixed))
    return (rows_ref[...].astype(F32) + gated).astype(BF16)


def middle_kernel(own_ref, other_ref, rows_ref, gain_ref, out_ref, block_ref):
    out = block_rows(own_ref, other_ref, rows_ref)
    out_ref[...] = out
    pack_block(out.astype(F32), gain_ref[...].astype(F32), block_ref)


def middle(own, other, rows, gain):
    return pl.pallas_call(
        middle_kernel,
        out_shape=(jax.ShapeDtypeStruct((F, T), BF16), jax.ShapeDtypeStruct((R, T), BF16)),
        in_specs=[vmem()] * 4,
        out_specs=(vmem(), vmem()),
        compiler_params=SMALL,
        name="middle",
    )(own, other, rows, gain)


def last_kernel(at_ref, own_ref, other_ref, rows_ref, head_ref, out_ref, swap_ref, stats_ref):
    out = block_rows(own_ref, other_ref, rows_ref)
    out_ref[...] = out
    @pl.when(at_ref[0] == 0)
    def _():
        swap_ref[...] = out

    @pl.when(at_ref[0] != 0)
    def _():
        swap_ref[...] = rows_ref[...]

    as_float = out.astype(F32)
    head = head_ref[...]
    squares = jnp.sum(as_float * as_float, axis=0, keepdims=True)
    scores = jnp.sum(as_float * head, axis=0, keepdims=True)
    stats = jnp.concatenate([squares, scores], axis=0)
    for i in range(32):
        stats_ref[i] = stats


def last(at, own, other, rows, head):
    out = jax.ShapeDtypeStruct((F, T), BF16)
    return pl.pallas_call(
        last_kernel,
        out_shape=(out, out, jax.ShapeDtypeStruct((32, 2, T), F32)),
        in_specs=[smem()] + [vmem()] * 4,
        out_specs=(vmem(), vmem(), vmem()),
        compiler_params=SMALL,
        name="last",
    )(at, own, other, rows, head)


def loss_kernel(stats_ref, label_ref, mask_ref, segment_ref, sums_ref):
    total = jnp.sum(stats_ref[...], axis=0)
    inv_root = lax.rsqrt(total[0:1] / D + EPS)
    score = total[1:2] * inv_root
    target = label_ref[...].astype(F32) - 1.0
    mask = mask_ref[...].astype(F32)
    err = score - target
    squared = mask * err * err
    member = segment_ref[...] == lax.broadcasted_iota(jnp.int32, (SEGS, T), 0)
    sums = jnp.sum(jnp.where(member, squared, 0.0), axis=1, keepdims=True)
    counts = jnp.sum(jnp.where(member, mask, 0.0), axis=1, keepdims=True)
    lane = lax.broadcasted_iota(jnp.int32, (SEGS, 128), 1)
    diagonal = lane == lax.broadcasted_iota(jnp.int32, (SEGS, 128), 0)
    sums = jnp.sum(jnp.where(diagonal, sums, 0.0), axis=0, keepdims=True)
    counts = jnp.sum(jnp.where(diagonal, counts, 0.0), axis=0, keepdims=True)
    both = jnp.concatenate([sums, counts], axis=0)
    for i in range(16):
        sums_ref[i] = both


def loss_parts(stats, label, mask, segment):
    return pl.pallas_call(
        loss_kernel,
        out_shape=jax.ShapeDtypeStruct((16, 2, 128), F32),
        in_specs=[vmem()] * 4,
        out_specs=vmem(),
        compiler_params=SMALL,
        name="loss_parts",
    )(stats, label, mask, segment)


def swapped(value, *axes):
    count = 2 ** len(axes)
    name = axes if len(axes) > 1 else axes[0]
    return lax.ppermute(value, name, [(i, i ^ (count - 1)) for i in range(count)])


def shifted(value, by):
    return lax.ppermute(value, Z, [(i, (i + by) % 16) for i in range(16)])


def gathered(block):
    same = lax.all_gather(block, "h", axis=0, tiled=False)
    return same, shifted(same[0:4], 1), shifted(same[4:8], -1)


def body(
    tokens_in, section_proj, section_gain, final_gain, score_weight, labels, loss_mask, segment_ids
):
    section = lax.axis_index("s")
    x = lax.axis_index("x")
    at = jnp.stack([section, x, x, lax.axis_index("p")]).astype(jnp.int32)
    weight = section_proj[0]

    gain = section_gain[0][:, None]
    gain_away = swapped(gain, "s")
    gain0 = jnp.where(section == 0, gain, gain_away)
    gain1 = jnp.where(section == 0, gain_away, gain)

    near, far = split(at, weight)
    near, far, gain0, gain1 = lax.optimization_barrier((near, far, gain0, gain1))
    blocks = (near, swapped(far, "x"), swapped(near, "s"), swapped(far, "s", "x"))

    rows = lax.dynamic_index_in_dim(tokens_in, section, 0, keepdims=False)
    same, below, above = gathered(pack(rows, gain0))

    own, send = product(0, at, same, below, above, blocks)
    first, block = middle(own, swapped(send, "x"), rows, gain1)

    same, below, above = gathered(block)
    own, send = product(1, at, same, below, above, blocks)
    head = (final_gain.astype(F32) * score_weight.astype(F32))[:, None]
    second, handed, stats = last(at, own, swapped(send, "x"), first, head)
    handed = swapped(handed, "s")

    stats = lax.all_to_all(stats, ("x", "h", "p"), 0, 0, tiled=True)
    pick = lambda value: lax.dynamic_slice(value, (section, 0), (1, T))
    parts = loss_parts(stats, pick(labels), pick(loss_mask), pick(segment_ids))
    parts = lax.all_to_all(parts, ("s", "y", "c"), 0, 0, tiled=True)
    parts = jnp.sum(parts.reshape(2, 8, 2, 128), axis=1)[:, :, :SEGS]
    segment_loss = parts[:, 0] / jnp.maximum(parts[:, 1], 1.0)

    section_out = jnp.where(section == 0, jnp.stack([first, handed]), jnp.stack([handed, second]))
    return section_out[None], segment_loss


def solution(mesh):
    finer = Mesh(mesh.devices.reshape(2, 4, 2, 2, 8, 2), ("s", "y", "c", "x", "h", "p"))
    tensor = ("x", "h", "p")
    dp = ("y", "c")
    in_specs = (
        P(None, tensor, dp),
        P("s", tensor, None),
        P("s", tensor),
        P(tensor),
        P(tensor),
        P(None, dp),
        P(None, dp),
        P(None, dp),
    )
    out_specs = (P("s", None, tensor, dp), P())
    return jax.shard_map(body, mesh=finer, in_specs=in_specs, out_specs=out_specs, check_vma=False)
```

```python
import functools

import jax
import jax.numpy as jnp
from jax import lax
from jax.experimental import pallas as pl
from jax.experimental.pallas import tpu as pltpu
from jax.sharding import Mesh
from jax.sharding import PartitionSpec as P

D = 7168
SEGS = 16
EPS = 1e-05
F = 224
T = 256
KH = D // 2
HALF = F // 2
R = 240
F32 = jnp.float32
BF16 = jnp.bfloat16
Z = ("h", "p")
SMALL = pltpu.CompilerParams(vmem_limit_bytes=4 * 1024 * 1024)
LARGE = pltpu.CompilerParams(vmem_limit_bytes=16 * 1024 * 1024)


def vmem():
    return pl.BlockSpec(memory_space=pltpu.VMEM)


def hbm():
    return pl.BlockSpec(memory_space=pltpu.HBM)


def anywhere():
    return pl.BlockSpec(memory_space=pl.ANY)


def column(row):
    down = lax.broadcasted_iota(jnp.int32, (F, F), 0)
    along = lax.broadcasted_iota(jnp.int32, (F, F), 1)
    wide = jnp.where(down == along, jnp.broadcast_to(row.astype(F32), (F, F)), 0.0)
    return jnp.sum(wide, axis=1, keepdims=True)


def picked(here_ref, away_ref, local):
    return column(jnp.where(local, here_ref[...].astype(F32), away_ref[...].astype(F32)))


def pack_block(rows, gain, block_ref):
    block_ref[0:F, :] = (rows * gain).astype(BF16)
    squares = jnp.sum(rows * rows, axis=0, keepdims=True)
    first = squares.astype(BF16)
    rest = squares - first.astype(F32)
    second = rest.astype(BF16)
    third = (rest - second.astype(F32)).astype(BF16)
    at = lax.broadcasted_iota(jnp.int32, (R - F, T), 0)
    tail = jnp.where(at == 0, first.astype(F32), 0.0)
    tail = jnp.where(at == 1, second.astype(F32), tail)
    tail = jnp.where(at == 2, third.astype(F32), tail)
    block_ref[F:R, :] = tail.astype(BF16)


def call(kernel, outs, ins, out_specs, params, name, scratch=()):
    return pl.pallas_call(
        kernel,
        out_shape=outs,
        in_specs=ins,
        out_specs=out_specs,
        scratch_shapes=scratch,
        compiler_params=params,
        name=name,
    )


def shape(dims, dtype):
    return jax.ShapeDtypeStruct(dims, dtype)


def pack_kernel(tokens_ref, here_ref, away_ref, block_ref):
    section = lax.axis_index("s")
    gain = picked(here_ref, away_ref, section == 0)
    pack_block(tokens_ref[section].astype(F32), gain, block_ref)


def pack(tokens, here, away):
    return call(
        pack_kernel, shape((R, T), BF16), [vmem()] * 3, vmem(), SMALL, "pack"
    )(tokens, here, away)


def split_kernel(weight_ref, near_ref, far_ref, sems):
    x = lax.axis_index("x")
    rows = pl.ds(pl.multiple_of(lax.axis_index("c") * HALF, 16), HALF)
    near = pl.ds(pl.multiple_of(x * KH, 128), KH)
    far = pl.ds(pl.multiple_of((1 - x) * KH, 128), KH)
    copies = [
        pltpu.make_async_copy(weight_ref.at[rows, near], near_ref, sems.at[0]),
        pltpu.make_async_copy(weight_ref.at[rows, far], far_ref, sems.at[1]),
    ]
    for copy in copies:
        copy.start()
    for copy in copies:
        copy.wait()


def split(weight):
    out = shape((HALF, KH), BF16)
    return call(
        split_kernel, (out, out), [hbm()], (anywhere(), anywhere()), SMALL, "split",
        [pltpu.SemaphoreType.DMA((2,))],
    )(weight)


def product_kernel(
    local_block, same_ref, below_ref, above_ref, weight_ref, side_ref, side2_ref, over_ref,
    over2_ref, cross_ref, cross2_ref, own_ref, send_ref, held, values, sems,
):
    local = lax.axis_index("s") == local_block
    parity = lax.axis_index("p")
    core = lax.axis_index("c")
    columns = pl.ds(pl.multiple_of(lax.axis_index("x") * KH, 128), KH)

    def rows(start, half):
        return pl.ds(pl.multiple_of(start + half * HALF, 16), HALF)

    def near_copies():
        return [
            pltpu.make_async_copy(weight_ref.at[:, columns], held.at[0:F, :], sems.at[0]),
            pltpu.make_async_copy(side_ref, held.at[rows(F, core), :], sems.at[1]),
            pltpu.make_async_copy(side2_ref, held.at[rows(F, 1 - core), :], sems.at[2]),
        ]

    def away_copies():
        return [
            pltpu.make_async_copy(over_ref, held.at[rows(0, core), :], sems.at[0]),
            pltpu.make_async_copy(over2_ref, held.at[rows(0, 1 - core), :], sems.at[1]),
            pltpu.make_async_copy(cross_ref, held.at[rows(F, core), :], sems.at[2]),
            pltpu.make_async_copy(cross2_ref, held.at[rows(F, 1 - core), :], sems.at[3]),
        ]

    @pl.when(local)
    def _():
        for copy in near_copies():
            copy.start()

    @pl.when(jnp.logical_not(local))
    def _():
        for copy in away_copies():
            copy.start()

    squares = jnp.zeros((1, T), F32)
    for i in range(8):
        got = same_ref[i]
        here = pl.ds(pl.multiple_of((2 * i + parity) * F, 16), F)
        values[here, :] = got[0:F]
        squares += jnp.sum(got[F:R].astype(F32), axis=0, keepdims=True)
        other = below_ref[i] if i < 4 else above_ref[i - 4]
        there = pl.ds(pl.multiple_of((2 * i + 1 - parity) * F, 16), F)
        values[there, :] = other[0:F]
        squares += jnp.sum(other[F:R].astype(F32), axis=0, keepdims=True)

    @pl.when(local)
    def _():
        for copy in near_copies():
            copy.wait()

    @pl.when(jnp.logical_not(local))
    def _():
        for copy in away_copies():
            copy.wait()

    product = jnp.dot(held[...], values[...], preferred_element_type=F32)
    total = jnp.broadcast_to(squares, (8, T))
    own_ref[0:F, :] = product[0:F]
    own_ref[F:F + 8, :] = total
    send_ref[0:F, :] = product[F:2 * F]
    send_ref[F:F + 8, :] = total


def product(local_block, same, below, above, blocks):
    out = shape((F + 8, T), F32)
    return call(
        functools.partial(product_kernel, local_block),
        (out, out),
        [vmem(), vmem(), vmem(), hbm()] + [anywhere()] * 6,
        (vmem(), vmem()),
        LARGE,
        "product",
        [
            pltpu.VMEM((2 * F, KH), BF16),
            pltpu.VMEM((KH, T), BF16),
            pltpu.SemaphoreType.DMA((4,)),
        ],
    )(same, below, above, *blocks)


def block_rows(own_ref, other_ref, rows):
    squares = own_ref[F:F + 1, :] + other_ref[F:F + 1, :]
    inv_root = lax.rsqrt(squares / D + EPS)
    mixed = (own_ref[0:F, :] + other_ref[0:F, :]) * inv_root
    gated = mixed / (1.0 + jnp.exp(-mixed))
    return (rows.astype(F32) + gated).astype(BF16)


def middle_kernel(own_ref, other_ref, tokens_ref, here_ref, away_ref, out_ref, block_ref):
    section = lax.axis_index("s")
    out = block_rows(own_ref, other_ref, tokens_ref[section])
    out_ref[...] = out
    gain = picked(here_ref, away_ref, section == 1)
    pack_block(out.astype(F32), gain, block_ref)


def middle(own, other, tokens, here, away):
    return call(
        middle_kernel,
        (shape((F, T), BF16), shape((R, T), BF16)),
        [vmem()] * 5,
        (vmem(), vmem()),
        SMALL,
        "middle",
    )(own, other, tokens, here, away)


def last_kernel(
    own_ref, other_ref, rows_ref, gain_ref, score_ref, out_ref, swap_ref, stats_ref
):
    out = block_rows(own_ref, other_ref, rows_ref[...])
    out_ref[...] = out
    section = lax.axis_index("s")

    @pl.when(section == 0)
    def _():
        swap_ref[...] = out

    @pl.when(section != 0)
    def _():
        swap_ref[...] = rows_ref[...]

    as_float = out.astype(F32)
    head = column(gain_ref[...].astype(F32) * score_ref[...].astype(F32))
    squares = jnp.sum(as_float * as_float, axis=0, keepdims=True)
    scores = jnp.sum(as_float * head, axis=0, keepdims=True)
    stats = jnp.concatenate([squares, scores], axis=0)
    for i in range(32):
        stats_ref[i] = stats


def last(own, other, rows, gain, score):
    out = shape((F, T), BF16)
    return call(
        last_kernel,
        (out, out, shape((32, 2, T), F32)),
        [vmem()] * 5,
        (vmem(), vmem(), vmem()),
        SMALL,
        "last",
    )(own, other, rows, gain, score)


def loss_kernel(stats_ref, label_ref, mask_ref, segment_ref, sums_ref):
    first = lax.axis_index("s") == 0

    def pick(ref):
        return jnp.where(first, ref[0:1, :], ref[1:2, :])

    total = jnp.sum(stats_ref[...], axis=0)
    inv_root = lax.rsqrt(total[0:1] / D + EPS)
    score = total[1:2] * inv_root
    target = pick(label_ref).astype(F32) - 1.0
    mask = pick(mask_ref).astype(F32)
    err = score - target
    squared = mask * err * err
    member = pick(segment_ref) == lax.broadcasted_iota(jnp.int32, (SEGS, T), 0)
    sums = jnp.sum(jnp.where(member, squared, 0.0), axis=1, keepdims=True)
    counts = jnp.sum(jnp.where(member, mask, 0.0), axis=1, keepdims=True)
    lane = lax.broadcasted_iota(jnp.int32, (SEGS, 128), 1)
    diagonal = lane == lax.broadcasted_iota(jnp.int32, (SEGS, 128), 0)
    sums = jnp.sum(jnp.where(diagonal, sums, 0.0), axis=0, keepdims=True)
    counts = jnp.sum(jnp.where(diagonal, counts, 0.0), axis=0, keepdims=True)
    both = jnp.concatenate([sums, counts], axis=0)
    for i in range(16):
        sums_ref[i] = both


def loss_parts(stats, label, mask, segment):
    return call(
        loss_kernel, shape((16, 2, 128), F32), [vmem()] * 4, vmem(), SMALL, "loss_parts"
    )(stats, label, mask, segment)


def swapped(value, *axes):
    count = 2 ** len(axes)
    name = axes if len(axes) > 1 else axes[0]
    return lax.ppermute(value, name, [(i, i ^ (count - 1)) for i in range(count)])


def shifted(value, by):
    return lax.ppermute(value, Z, [(i, (i + by) % 16) for i in range(16)])


def body(
    tokens_in, section_proj, section_gain, final_gain, score_weight, labels, loss_mask, segment_ids
):
    section = lax.axis_index("s")
    weight = section_proj[0]
    gain_away = swapped(section_gain, "s")

    near, far = split(weight)
    near, far, gain_away = lax.optimization_barrier((near, far, gain_away))
    side = swapped(far, "x")
    over = swapped(near, "s")
    cross = swapped(far, "s", "x")

    same = lax.all_gather(pack(tokens_in, section_gain, gain_away), "h", axis=0, tiled=False)
    low, high = same[0:4], same[4:8]
    low, high, side, over, cross = lax.optimization_barrier((low, high, side, over, cross))
    below, above = shifted(low, 1), shifted(high, -1)
    blocks = (
        weight, side, swapped(side, "c"), over, swapped(over, "c"), cross, swapped(cross, "c")
    )
    own, send = product(0, same, below, above, blocks)
    first, block = middle(own, swapped(send, "x"), tokens_in, section_gain, gain_away)

    same = lax.all_gather(block, "h", axis=0, tiled=False)
    below, above = shifted(same[0:4], 1), shifted(same[4:8], -1)
    own, send = product(1, same, below, above, blocks)
    second, handed, stats = last(
        own, swapped(send, "x"), first, final_gain[None], score_weight[None]
    )
    handed = swapped(handed, "s")

    stats = lax.all_to_all(stats, ("x", "h", "p"), 0, 0, tiled=True)
    parts = loss_parts(stats, labels, loss_mask, segment_ids)
    parts = lax.all_to_all(parts, ("s", "y", "c"), 0, 0, tiled=True)
    parts = jnp.sum(parts.reshape(2, 8, 2, 128), axis=1)[:, :, :SEGS]
    segment_loss = parts[:, 0] / jnp.maximum(parts[:, 1], 1.0)

    section_out = jnp.where(section == 0, jnp.stack([first, handed]), jnp.stack([handed, second]))
    return section_out[None], segment_loss


def solution(mesh):
    finer = Mesh(mesh.devices.reshape(2, 4, 2, 2, 8, 2), ("s", "y", "c", "x", "h", "p"))
    tensor = ("x", "h", "p")
    dp = ("y", "c")
    in_specs = (
        P(None, tensor, dp),
        P("s", tensor, None),
        P("s", tensor),
        P(tensor),
        P(tensor),
        P(None, dp),
        P(None, dp),
        P(None, dp),
    )
    out_specs = (P("s", None, tensor, dp), P())
    return jax.shard_map(body, mesh=finer, in_specs=in_specs, out_specs=out_specs, check_vma=False)
```

```python
import jax
import jax.numpy as jnp
from jax import lax
from jax.experimental import pallas as pl
from jax.experimental.pallas import tpu as pltpu
from jax.sharding import Mesh
from jax.sharding import PartitionSpec as P

D = 7168
SEGS = 16
EPS = 1e-05
F = 224
T = 256
KH = D // 2
HALF = F // 2
R = 240
F32 = jnp.float32
BF16 = jnp.bfloat16
SCALE = 32.0
SMALL = pltpu.CompilerParams(vmem_limit_bytes=4 * 1024 * 1024)
MEDIUM = pltpu.CompilerParams(vmem_limit_bytes=8 * 1024 * 1024)
LARGE = pltpu.CompilerParams(vmem_limit_bytes=12 * 1024 * 1024)


def vmem():
    return pl.BlockSpec(memory_space=pltpu.VMEM)


def anywhere():
    return pl.BlockSpec(memory_space=pl.ANY)


def column(row):
    down = lax.broadcasted_iota(jnp.int32, (F, F), 0)
    along = lax.broadcasted_iota(jnp.int32, (F, F), 1)
    wide = jnp.where(down == along, jnp.broadcast_to(row.astype(F32), (F, F)), 0.0)
    return jnp.sum(wide, axis=1, keepdims=True)


def picked(here_ref, away_ref, local):
    return column(jnp.where(local, here_ref[...].astype(F32), away_ref[...].astype(F32)))


def pack_block(rows, gain, block_ref):
    block_ref[0:F, :] = ((rows * gain).astype(BF16).astype(F32) * SCALE).astype(BF16)
    block_ref[F:R, :] = three_terms(jnp.sqrt(jnp.sum(rows * rows, axis=0, keepdims=True)))


def call(kernel, outs, ins, out_specs, params, name, scratch=()):
    return pl.pallas_call(
        kernel,
        out_shape=outs,
        in_specs=ins,
        out_specs=out_specs,
        scratch_shapes=scratch,
        compiler_params=params,
        name=name,
    )


def shape(dims, dtype):
    return jax.ShapeDtypeStruct(dims, dtype)


def pack_kernel(tokens_ref, here_ref, away_ref, block_ref):
    section = lax.axis_index("s")
    gain = picked(here_ref, away_ref, section == 0)
    pack_block(tokens_ref[section].astype(F32), gain, block_ref)


def pack(tokens, here, away):
    return call(
        pack_kernel, shape((R, T), BF16), [vmem()] * 3, vmem(), SMALL, "pack"
    )(tokens, here, away)


def split_kernel(weight_ref, out_ref, sems):
    rows = pl.ds(pl.multiple_of(lax.axis_index("c") * HALF, 16), HALF)
    copies = []
    for i in range(4):
        columns = pl.ds(i % 2 * KH, KH)
        copies.append(
            pltpu.make_async_copy(weight_ref.at[rows, columns], out_ref.at[i], sems.at[i])
        )
    for copy in copies:
        copy.start()
    for copy in copies:
        copy.wait()


def split(weight):
    return call(
        split_kernel, shape((4, HALF, KH), BF16), [anywhere()], vmem(), MEDIUM, "split",
        [pltpu.SemaphoreType.DMA((4,))],
    )(weight)


def three_terms(row):
    first = row.astype(BF16)
    rest = row - first.astype(F32)
    second = rest.astype(BF16)
    third = (rest - second.astype(F32)).astype(BF16)
    at = lax.broadcasted_iota(jnp.int32, (R - F, T), 0)
    tail = jnp.where(at == 0, first.astype(F32), 0.0)
    tail = jnp.where(at == 1, second.astype(F32), tail)
    tail = jnp.where(at == 2, third.astype(F32), tail)
    return tail.astype(BF16)


def product_kernel(
    same_ref, half_ref, half2_ref, own_ref, send_ref, held, values, sems
):
    core = lax.axis_index("c")
    x = lax.axis_index("x")
    copies = []
    for i in range(4):
        ref, half = (half_ref, core) if i % 2 == 0 else (half2_ref, 1 - core)
        index, start = (x, 0) if i < 2 else (1 - x, F)
        rows = pl.ds(pl.multiple_of(start + half * HALF, 16), HALF)
        copies.append(pltpu.make_async_copy(ref.at[index], held.at[rows, :], sems.at[i]))
    for copy in copies:
        copy.start()

    squares = jnp.zeros((1, T), F32)
    for i in range(16):
        got = same_ref[i]
        values[i * F:(i + 1) * F, :] = got[0:F]
        root = jnp.sum(got[F:R].astype(F32), axis=0, keepdims=True)
        squares += root * root

    for copy in copies:
        copy.wait()

    product = jnp.dot(held[...], values[...], preferred_element_type=F32)
    own_ref[0:F, :] = product[0:F]
    own_ref[F:F + 8, :] = jnp.broadcast_to(squares, (8, T))
    send_ref[0:F, :] = product[F:2 * F].astype(BF16)
    send_ref[F:R, :] = three_terms(squares)


def product(same, halves):
    return call(
        product_kernel,
        (shape((F + 8, T), F32), shape((R, T), BF16)),
        [vmem(), anywhere(), anywhere()],
        (vmem(), vmem()),
        LARGE,
        "product",
        [
            pltpu.VMEM((2 * F, KH), BF16),
            pltpu.VMEM((KH, T), BF16),
            pltpu.SemaphoreType.DMA((4,)),
        ],
    )(same, *halves)


def block_rows(own_ref, other_ref, rows):
    other = jnp.sum(other_ref[F:R, :].astype(F32), axis=0, keepdims=True)
    inv_root = lax.rsqrt((own_ref[F:F + 1, :] + other) / D + EPS) / SCALE
    mixed = (own_ref[0:F, :] + other_ref[0:F, :].astype(F32)) * inv_root
    gated = mixed / (1.0 + jnp.exp(-mixed))
    return (rows.astype(F32) + gated).astype(BF16)


def middle_kernel(own_ref, other_ref, tokens_ref, here_ref, away_ref, out_ref, block_ref):
    section = lax.axis_index("s")
    out = block_rows(own_ref, other_ref, tokens_ref[section])
    out_ref[...] = out
    gain = picked(here_ref, away_ref, section == 1)
    pack_block(out.astype(F32), gain, block_ref)


def middle(own, other, tokens, here, away):
    return call(
        middle_kernel,
        (shape((F, T), BF16), shape((R, T), BF16)),
        [vmem()] * 5,
        (vmem(), vmem()),
        SMALL,
        "middle",
    )(own, other, tokens, here, away)


def last_kernel(
    own_ref, other_ref, rows_ref, gain_ref, score_ref, out_ref, swap_ref, stats_ref
):
    out = block_rows(own_ref, other_ref, rows_ref[...])
    out_ref[...] = out
    section = lax.axis_index("s")

    @pl.when(section == 0)
    def _():
        swap_ref[...] = out

    @pl.when(section != 0)
    def _():
        swap_ref[...] = rows_ref[...]

    as_float = out.astype(F32)
    head = column(gain_ref[...].astype(F32) * score_ref[...].astype(F32))
    squares = jnp.sum(as_float * as_float, axis=0, keepdims=True)
    scores = jnp.sum(as_float * head, axis=0, keepdims=True)
    stats = jnp.concatenate([squares, scores], axis=0)
    for i in range(32):
        stats_ref[i] = stats


def last(own, other, rows, gain, score):
    out = shape((F, T), BF16)
    return call(
        last_kernel,
        (out, out, shape((32, 2, T), F32)),
        [vmem()] * 5,
        (vmem(), vmem(), vmem()),
        SMALL,
        "last",
    )(own, other, rows, gain, score)


def loss_kernel(stats_ref, label_ref, mask_ref, segment_ref, sums_ref):
    first = lax.axis_index("s") == 0

    def pick(ref):
        return jnp.where(first, ref[0:1, :], ref[1:2, :])

    total = jnp.sum(stats_ref[...], axis=0)
    inv_root = lax.rsqrt(total[0:1] / D + EPS)
    score = total[1:2] * inv_root
    target = pick(label_ref).astype(F32) - 1.0
    mask = pick(mask_ref).astype(F32)
    err = score - target
    squared = mask * err * err
    member = pick(segment_ref) == lax.broadcasted_iota(jnp.int32, (SEGS, T), 0)
    sums = jnp.sum(jnp.where(member, squared, 0.0), axis=1, keepdims=True)
    counts = jnp.sum(jnp.where(member, mask, 0.0), axis=1, keepdims=True)
    lane = lax.broadcasted_iota(jnp.int32, (SEGS, 128), 1)
    diagonal = lane == lax.broadcasted_iota(jnp.int32, (SEGS, 128), 0)
    sums = jnp.sum(jnp.where(diagonal, sums, 0.0), axis=0, keepdims=True)
    counts = jnp.sum(jnp.where(diagonal, counts, 0.0), axis=0, keepdims=True)
    both = jnp.concatenate([sums, counts], axis=0)
    for i in range(16):
        sums_ref[i] = both


def loss_parts(stats, label, mask, segment):
    return call(
        loss_kernel, shape((16, 2, 128), F32), [vmem()] * 4, vmem(), SMALL, "loss_parts"
    )(stats, label, mask, segment)


def swapped(value, *axes):
    count = 2 ** len(axes)
    name = axes if len(axes) > 1 else axes[0]
    return lax.ppermute(value, name, [(i, i ^ (count - 1)) for i in range(count)])


def gathered(block):
    return lax.all_gather(block.astype(jnp.float16), "z", axis=0, tiled=False).astype(BF16)


def body(
    tokens_in, section_proj, section_gain, final_gain, score_weight, labels, loss_mask, segment_ids
):
    section = lax.axis_index("s")
    gain_away = swapped(section_gain, "s")

    pieces, gain_away = lax.optimization_barrier((split(section_proj[0]), gain_away))
    half = lax.all_to_all(pieces, ("s", "x"), 0, 0, tiled=True)

    same = gathered(pack(tokens_in, section_gain, gain_away))
    same, half = lax.optimization_barrier((same, half))
    near = half[0:2]
    own, send = product(same, (near, swapped(near, "c")))
    send, half = lax.optimization_barrier((send, half))
    away = half[2:4]
    away2 = swapped(away, "c")
    first, block = middle(own, swapped(send, "x"), tokens_in, section_gain, gain_away)

    own, send = product(gathered(block), (away, away2))
    second, handed, stats = last(
        own, swapped(send, "x"), first, final_gain[None], score_weight[None]
    )
    handed = swapped(handed, "s")

    stats = lax.all_to_all(stats, ("x", "z"), 0, 0, tiled=True)
    parts = loss_parts(stats, labels, loss_mask, segment_ids)
    parts = lax.all_to_all(parts, ("s", "y", "c"), 0, 0, tiled=True)
    parts = jnp.sum(parts.reshape(2, 8, 2, 128), axis=1)[:, :, :SEGS]
    segment_loss = parts[:, 0] / jnp.maximum(parts[:, 1], 1.0)

    section_out = jnp.where(section == 0, jnp.stack([first, handed]), jnp.stack([handed, second]))
    return section_out[None], segment_loss


def solution(mesh):
    finer = Mesh(mesh.devices.reshape(2, 4, 2, 2, 16), ("s", "y", "c", "x", "z"))
    tensor = ("x", "z")
    dp = ("y", "c")
    in_specs = (
        P(None, tensor, dp),
        P("s", tensor, None),
        P("s", tensor),
        P(tensor),
        P(tensor),
        P(None, dp),
        P(None, dp),
        P(None, dp),
    )
    out_specs = (P("s", None, tensor, dp), P())
    return jax.shard_map(body, mesh=finer, in_specs=in_specs, out_specs=out_specs, check_vma=False)
```

```python
import functools

import jax
import jax.numpy as jnp
from jax import lax
from jax.experimental import pallas as pl
from jax.experimental.pallas import tpu as pltpu
from jax.sharding import Mesh
from jax.sharding import PartitionSpec as P

D = 7168
SEGS = 16
EPS = 1e-05
F = 224
T = 256
KH = D // 2
HALF = F // 2
R = 232
F32 = jnp.float32
BF16 = jnp.bfloat16
SCALE = 32.0
SMALL = pltpu.CompilerParams(vmem_limit_bytes=4 * 1024 * 1024)
WHOLE = pltpu.CompilerParams(vmem_limit_bytes=60 * 1024 * 1024)
LARGE = pltpu.CompilerParams(vmem_limit_bytes=12 * 1024 * 1024)


def vmem():
    return pl.BlockSpec(memory_space=pltpu.VMEM)


def anywhere():
    return pl.BlockSpec(memory_space=pl.ANY)


def column(row):
    down = lax.broadcasted_iota(jnp.int32, (F, F), 0)
    along = lax.broadcasted_iota(jnp.int32, (F, F), 1)
    wide = jnp.where(down == along, jnp.broadcast_to(row.astype(F32), (F, F)), 0.0)
    return jnp.sum(wide, axis=1, keepdims=True)


def picked(here_ref, away_ref, local):
    return column(jnp.where(local, here_ref[...].astype(F32), away_ref[...].astype(F32)))


def pack_block(rows, gain, block_ref):
    block_ref[0:F, :] = ((rows * gain).astype(BF16).astype(F32) * SCALE).astype(BF16)
    block_ref[F:R, :] = three_terms(jnp.sqrt(jnp.sum(rows * rows, axis=0, keepdims=True)))


def call(kernel, outs, ins, out_specs, params, name, scratch=()):
    return pl.pallas_call(
        kernel,
        out_shape=outs,
        in_specs=ins,
        out_specs=out_specs,
        scratch_shapes=scratch,
        compiler_params=params,
        name=name,
    )


def shape(dims, dtype):
    return jax.ShapeDtypeStruct(dims, dtype)


def pack_kernel(tokens_ref, here_ref, away_ref, block_ref):
    section = lax.axis_index("s")
    gain = picked(here_ref, away_ref, section == 0)
    pack_block(tokens_ref[section].astype(F32), gain, block_ref)


def pack(tokens, here, away):
    return call(
        pack_kernel, shape((R, T), BF16), [vmem()] * 3, vmem(), SMALL, "pack"
    )(tokens, here, away)


def split_kernel(weight_ref, out_ref, held, sems):
    rows = pl.ds(pl.multiple_of(lax.axis_index("c") * HALF, 16), HALF)
    loads = []
    for i in range(2):
        columns = pl.ds(i * KH, KH)
        loads.append(
            pltpu.make_async_copy(weight_ref.at[rows, columns], held.at[i], sems.at[4 + i])
        )
    stores = [pltpu.make_async_copy(held.at[i % 2], out_ref.at[i], sems.at[i]) for i in range(4)]
    for load in loads:
        load.start()
    for i in range(2):
        loads[i].wait()
        stores[i].start()
        stores[i + 2].start()
    for store in stores:
        store.wait()


def split(weight):
    return call(
        split_kernel, shape((4, HALF, KH), BF16), [anywhere()], anywhere(), WHOLE, "split",
        [pltpu.VMEM((2, HALF, KH), BF16), pltpu.SemaphoreType.DMA((6,))],
    )(weight)


def three_terms(row):
    first = row.astype(BF16)
    rest = row - first.astype(F32)
    second = rest.astype(BF16)
    third = (rest - second.astype(F32)).astype(BF16)
    at = lax.broadcasted_iota(jnp.int32, (R - F, T), 0)
    tail = jnp.where(at == 0, first.astype(F32), 0.0)
    tail = jnp.where(at == 1, second.astype(F32), tail)
    tail = jnp.where(at == 2, third.astype(F32), tail)
    return tail.astype(BF16)


def product_kernel(
    block, same_ref, half_ref, half2_ref, own_ref, send_ref, held, values, sems
):
    core = lax.axis_index("c")
    x = lax.axis_index("x")
    copies = []
    for i in range(4):
        ref, half = (half_ref, core) if i % 2 == 0 else (half2_ref, 1 - core)
        index, start = (2 * block + x, 0) if i < 2 else (2 * block + 1 - x, F)
        rows = pl.ds(pl.multiple_of(start + half * HALF, 16), HALF)
        copies.append(pltpu.make_async_copy(ref.at[index], held.at[rows, :], sems.at[i]))
    for copy in copies:
        copy.start()

    squares = jnp.zeros((1, T), F32)
    for i in range(16):
        got = same_ref[i]
        values[i * F:(i + 1) * F, :] = got[0:F]
        root = jnp.sum(got[F:R].astype(F32), axis=0, keepdims=True)
        squares += root * root

    for copy in copies:
        copy.wait()

    product = jnp.dot(held[...], values[...], preferred_element_type=F32)
    own_ref[0:F, :] = product[0:F]
    own_ref[F:F + 8, :] = jnp.broadcast_to(squares, (8, T))
    send_ref[0:F, :] = product[F:2 * F].astype(BF16)
    send_ref[F:R, :] = three_terms(squares)


def product(block, same, halves):
    return call(
        functools.partial(product_kernel, block),
        (shape((F + 8, T), F32), shape((R, T), BF16)),
        [vmem(), anywhere(), anywhere()],
        (vmem(), vmem()),
        LARGE,
        "product",
        [
            pltpu.VMEM((2 * F, KH), BF16),
            pltpu.VMEM((KH, T), BF16),
            pltpu.SemaphoreType.DMA((4,)),
        ],
    )(same, *halves)


def block_rows(own_ref, other_ref, rows):
    other = jnp.sum(other_ref[F:R, :].astype(F32), axis=0, keepdims=True)
    inv_root = lax.rsqrt((own_ref[F:F + 1, :] + other) / D + EPS) / SCALE
    mixed = (own_ref[0:F, :] + other_ref[0:F, :].astype(F32)) * inv_root
    gated = mixed / (1.0 + jnp.exp(-mixed))
    return (rows.astype(F32) + gated).astype(BF16)


def middle_kernel(own_ref, other_ref, tokens_ref, here_ref, away_ref, out_ref, block_ref):
    section = lax.axis_index("s")
    out = block_rows(own_ref, other_ref, tokens_ref[section])
    out_ref[...] = out
    gain = picked(here_ref, away_ref, section == 1)
    pack_block(out.astype(F32), gain, block_ref)


def middle(own, other, tokens, here, away):
    return call(
        middle_kernel,
        (shape((F, T), BF16), shape((R, T), BF16)),
        [vmem()] * 5,
        (vmem(), vmem()),
        SMALL,
        "middle",
    )(own, other, tokens, here, away)


def last_kernel(
    own_ref, other_ref, rows_ref, gain_ref, score_ref, out_ref, swap_ref, stats_ref
):
    out = block_rows(own_ref, other_ref, rows_ref[...])
    out_ref[...] = out
    section = lax.axis_index("s")

    @pl.when(section == 0)
    def _():
        swap_ref[...] = out

    @pl.when(section != 0)
    def _():
        swap_ref[...] = rows_ref[...]

    as_float = out.astype(F32)
    head = column(gain_ref[...].astype(F32) * score_ref[...].astype(F32))
    squares = jnp.sum(as_float * as_float, axis=0, keepdims=True)
    scores = jnp.sum(as_float * head, axis=0, keepdims=True)
    stats = jnp.concatenate([squares, scores], axis=0)
    for i in range(32):
        stats_ref[i] = stats


def last(own, other, rows, gain, score):
    out = shape((F, T), BF16)
    return call(
        last_kernel,
        (out, out, shape((32, 2, T), F32)),
        [vmem()] * 5,
        (vmem(), vmem(), vmem()),
        SMALL,
        "last",
    )(own, other, rows, gain, score)


def loss_kernel(stats_ref, label_ref, mask_ref, segment_ref, sums_ref):
    first = lax.axis_index("s") == 0

    def pick(ref):
        return jnp.where(first, ref[0:1, :], ref[1:2, :])

    total = jnp.sum(stats_ref[...], axis=0)
    inv_root = lax.rsqrt(total[0:1] / D + EPS)
    score = total[1:2] * inv_root
    target = pick(label_ref).astype(F32) - 1.0
    mask = pick(mask_ref).astype(F32)
    err = score - target
    squared = mask * err * err
    member = pick(segment_ref) == lax.broadcasted_iota(jnp.int32, (SEGS, T), 0)
    sums = jnp.sum(jnp.where(member, squared, 0.0), axis=1, keepdims=True)
    counts = jnp.sum(jnp.where(member, mask, 0.0), axis=1, keepdims=True)
    lane = lax.broadcasted_iota(jnp.int32, (SEGS, 128), 1)
    diagonal = lane == lax.broadcasted_iota(jnp.int32, (SEGS, 128), 0)
    sums = jnp.sum(jnp.where(diagonal, sums, 0.0), axis=0, keepdims=True)
    counts = jnp.sum(jnp.where(diagonal, counts, 0.0), axis=0, keepdims=True)
    both = jnp.concatenate([sums, counts], axis=0)
    for i in range(16):
        sums_ref[i] = both


def loss_parts(stats, label, mask, segment):
    return call(
        loss_kernel, shape((16, 2, 128), F32), [vmem()] * 4, vmem(), SMALL, "loss_parts"
    )(stats, label, mask, segment)


def swapped(value, *axes):
    count = 2 ** len(axes)
    name = axes if len(axes) > 1 else axes[0]
    return lax.ppermute(value, name, [(i, i ^ (count - 1)) for i in range(count)])


def gathered(block):
    return lax.all_gather(block.astype(jnp.float16), "z", axis=0, tiled=False)


def body(
    tokens_in, section_proj, section_gain, final_gain, score_weight, labels, loss_mask, segment_ids
):
    section = lax.axis_index("s")
    gain_away = swapped(section_gain, "s")

    pieces, gain_away = lax.optimization_barrier((split(section_proj[0]), gain_away))
    half = lax.all_to_all(pieces, ("s", "x"), 0, 0, tiled=True)

    same = gathered(pack(tokens_in, section_gain, gain_away))
    same, half = lax.optimization_barrier((same, half))
    halves = half, swapped(half, "c")
    own, send = product(0, same.astype(BF16), halves)
    first, block = middle(own, swapped(send, "x"), tokens_in, section_gain, gain_away)

    own, send = product(1, gathered(block).astype(BF16), halves)
    second, handed, stats = last(
        own, swapped(send, "x"), first, final_gain[None], score_weight[None]
    )
    handed = swapped(handed, "s")

    stats = lax.all_to_all(stats, ("x", "z"), 0, 0, tiled=True)
    parts = loss_parts(stats, labels, loss_mask, segment_ids)
    parts = lax.all_to_all(parts, ("s", "y", "c"), 0, 0, tiled=True)
    parts = jnp.sum(parts.reshape(2, 8, 2, 128), axis=1)[:, :, :SEGS]
    segment_loss = parts[:, 0] / jnp.maximum(parts[:, 1], 1.0)

    section_out = jnp.where(section == 0, jnp.stack([first, handed]), jnp.stack([handed, second]))
    return section_out[None], segment_loss


def solution(mesh):
    finer = Mesh(mesh.devices.reshape(2, 4, 2, 2, 16), ("s", "y", "c", "x", "z"))
    tensor = ("x", "z")
    dp = ("y", "c")
    in_specs = (
        P(None, tensor, dp),
        P("s", tensor, None),
        P("s", tensor),
        P(tensor),
        P(tensor),
        P(None, dp),
        P(None, dp),
        P(None, dp),
    )
    out_specs = (P("s", None, tensor, dp), P())
    return jax.shard_map(body, mesh=finer, in_specs=in_specs, out_specs=out_specs, check_vma=False)
```

```python
import functools

import jax
import jax.numpy as jnp
from jax import lax
from jax.experimental import pallas as pl
from jax.experimental.pallas import tpu as pltpu
from jax.sharding import Mesh
from jax.sharding import PartitionSpec as P

D = 7168
SEGS = 16
EPS = 1e-05
F = 224
T = 256
KH = D // 2
HALF = F // 2
R = 232
F32 = jnp.float32
BF16 = jnp.bfloat16
SCALE = 32.0
SMALL = pltpu.CompilerParams(vmem_limit_bytes=4 * 1024 * 1024)
WHOLE = pltpu.CompilerParams(vmem_limit_bytes=60 * 1024 * 1024)
LARGE = pltpu.CompilerParams(vmem_limit_bytes=12 * 1024 * 1024)


def vmem():
    return pl.BlockSpec(memory_space=pltpu.VMEM)


def anywhere():
    return pl.BlockSpec(memory_space=pl.ANY)


def column(row):
    down = lax.broadcasted_iota(jnp.int32, (F, F), 0)
    along = lax.broadcasted_iota(jnp.int32, (F, F), 1)
    wide = jnp.where(down == along, jnp.broadcast_to(row.astype(F32), (F, F)), 0.0)
    return jnp.sum(wide, axis=1, keepdims=True)


def picked(here_ref, away_ref, local):
    return column(jnp.where(local, here_ref[...].astype(F32), away_ref[...].astype(F32)))


def pack_block(rows, gain, block_ref):
    block_ref[0:F, :] = ((rows * gain).astype(BF16).astype(F32) * SCALE).astype(BF16)
    block_ref[F:R, :] = three_terms(jnp.sqrt(jnp.sum(rows * rows, axis=0, keepdims=True)))


def call(kernel, outs, ins, out_specs, params, name, scratch=()):
    return pl.pallas_call(
        kernel,
        out_shape=outs,
        in_specs=ins,
        out_specs=out_specs,
        scratch_shapes=scratch,
        compiler_params=params,
        name=name,
    )


def shape(dims, dtype):
    return jax.ShapeDtypeStruct(dims, dtype)


def pack_kernel(tokens_ref, here_ref, away_ref, block_ref):
    section = lax.axis_index("s")
    gain = picked(here_ref, away_ref, section == 0)
    pack_block(tokens_ref[section].astype(F32), gain, block_ref)


def pack(tokens, here, away):
    return call(
        pack_kernel, shape((R, T), BF16), [vmem()] * 3, vmem(), SMALL, "pack"
    )(tokens, here, away)


def split_kernel(weight_ref, out_ref, held, sems):
    rows = pl.ds(pl.multiple_of(lax.axis_index("c") * HALF, 16), HALF)
    loads = []
    for i in range(2):
        columns = pl.ds(i * KH, KH)
        loads.append(
            pltpu.make_async_copy(weight_ref.at[rows, columns], held.at[i], sems.at[4 + i])
        )
    stores = [pltpu.make_async_copy(held.at[i % 2], out_ref.at[i], sems.at[i]) for i in range(4)]
    for load in loads:
        load.start()
    for i in range(2):
        loads[i].wait()
        stores[i].start()
        stores[i + 2].start()
    for store in stores:
        store.wait()


def split(weight):
    return call(
        split_kernel, shape((4, HALF, KH), BF16), [anywhere()], anywhere(), WHOLE, "split",
        [pltpu.VMEM((2, HALF, KH), BF16), pltpu.SemaphoreType.DMA((6,))],
    )(weight)


def three_terms(row):
    first = row.astype(BF16)
    rest = row - first.astype(F32)
    second = rest.astype(BF16)
    third = (rest - second.astype(F32)).astype(BF16)
    at = lax.broadcasted_iota(jnp.int32, (R - F, T), 0)
    tail = jnp.where(at == 0, first.astype(F32), 0.0)
    tail = jnp.where(at == 1, second.astype(F32), tail)
    tail = jnp.where(at == 2, third.astype(F32), tail)
    return tail.astype(BF16)


def product_kernel(
    block, same_ref, half_ref, half2_ref, own_ref, send_ref, held, values, sems
):
    core = lax.axis_index("c")
    x = lax.axis_index("x")
    copies = []
    for i in range(4):
        ref, half = (half_ref, core) if i % 2 == 0 else (half2_ref, 1 - core)
        index, start = (2 * block + x, 0) if i < 2 else (2 * block + 1 - x, F)
        rows = pl.ds(pl.multiple_of(start + half * HALF, 16), HALF)
        copies.append(pltpu.make_async_copy(ref.at[index], held.at[rows, :], sems.at[i]))
    for copy in copies:
        copy.start()

    squares = jnp.zeros((1, T), F32)
    for i in range(16):
        got = same_ref[i]
        values[i * F:(i + 1) * F, :] = got[0:F]
        root = jnp.sum(got[F:R].astype(F32), axis=0, keepdims=True)
        squares += root * root

    for copy in copies:
        copy.wait()

    product = jnp.dot(held[...], values[...], preferred_element_type=F32)
    own_ref[0:F, :] = product[0:F]
    own_ref[F:F + 8, :] = jnp.broadcast_to(squares, (8, T))
    send_ref[0:F, :] = product[F:2 * F].astype(BF16)
    send_ref[F:R, :] = three_terms(squares)


def product(block, same, halves):
    return call(
        functools.partial(product_kernel, block),
        (shape((F + 8, T), F32), shape((R, T), BF16)),
        [vmem(), anywhere(), anywhere()],
        (vmem(), vmem()),
        LARGE,
        "product",
        [
            pltpu.VMEM((2 * F, KH), BF16),
            pltpu.VMEM((KH, T), BF16),
            pltpu.SemaphoreType.DMA((4,)),
        ],
    )(same, *halves)


def block_rows(own_ref, pair_ref, rows):
    sent = pair_ref[1 - lax.axis_index("x")].astype(F32)
    other = jnp.sum(sent[F:R], axis=0, keepdims=True)
    inv_root = lax.rsqrt((own_ref[F:F + 1, :] + other) / D + EPS) / SCALE
    mixed = (own_ref[0:F, :] + sent[0:F]) * inv_root
    gated = mixed / (1.0 + jnp.exp(-mixed))
    return (rows.astype(F32) + gated).astype(BF16)


def middle_kernel(own_ref, pair_ref, tokens_ref, here_ref, away_ref, out_ref, block_ref):
    section = lax.axis_index("s")
    out = block_rows(own_ref, pair_ref, tokens_ref[section])
    out_ref[...] = out
    gain = picked(here_ref, away_ref, section == 1)
    pack_block(out.astype(F32), gain, block_ref)


def middle(own, pair, tokens, here, away):
    return call(
        middle_kernel,
        (shape((F, T), BF16), shape((R, T), BF16)),
        [vmem()] * 5,
        (vmem(), vmem()),
        SMALL,
        "middle",
    )(own, pair, tokens, here, away)


def last_kernel(
    own_ref, pair_ref, rows_ref, gain_ref, score_ref, out_ref, swap_ref, stats_ref
):
    out = block_rows(own_ref, pair_ref, rows_ref[...])
    out_ref[...] = out
    section = lax.axis_index("s")

    @pl.when(section == 0)
    def _():
        swap_ref[...] = out

    @pl.when(section != 0)
    def _():
        swap_ref[...] = rows_ref[...]

    as_float = out.astype(F32)
    head = column(gain_ref[...].astype(F32) * score_ref[...].astype(F32))
    squares = jnp.sum(as_float * as_float, axis=0, keepdims=True)
    scores = jnp.sum(as_float * head, axis=0, keepdims=True)
    stats = jnp.concatenate([squares, scores], axis=0)
    for i in range(32):
        stats_ref[i] = stats


def last(own, pair, rows, gain, score):
    out = shape((F, T), BF16)
    return call(
        last_kernel,
        (out, out, shape((32, 2, T), F32)),
        [vmem()] * 5,
        (vmem(), vmem(), vmem()),
        SMALL,
        "last",
    )(own, pair, rows, gain, score)


def loss_kernel(stats_ref, label_ref, mask_ref, segment_ref, sums_ref):
    first = lax.axis_index("s") == 0

    def pick(ref):
        return jnp.where(first, ref[0:1, :], ref[1:2, :])

    total = jnp.sum(stats_ref[...], axis=0)
    inv_root = lax.rsqrt(total[0:1] / D + EPS)
    score = total[1:2] * inv_root
    target = pick(label_ref).astype(F32) - 1.0
    mask = pick(mask_ref).astype(F32)
    err = score - target
    squared = mask * err * err
    member = pick(segment_ref) == lax.broadcasted_iota(jnp.int32, (SEGS, T), 0)
    sums = jnp.sum(jnp.where(member, squared, 0.0), axis=1, keepdims=True)
    counts = jnp.sum(jnp.where(member, mask, 0.0), axis=1, keepdims=True)
    lane = lax.broadcasted_iota(jnp.int32, (SEGS, 128), 1)
    diagonal = lane == lax.broadcasted_iota(jnp.int32, (SEGS, 128), 0)
    sums = jnp.sum(jnp.where(diagonal, sums, 0.0), axis=0, keepdims=True)
    counts = jnp.sum(jnp.where(diagonal, counts, 0.0), axis=0, keepdims=True)
    both = jnp.concatenate([sums, counts], axis=0)
    for i in range(16):
        sums_ref[i] = both


def loss_parts(stats, label, mask, segment):
    return call(
        loss_kernel, shape((16, 2, 128), F32), [vmem()] * 4, vmem(), SMALL, "loss_parts"
    )(stats, label, mask, segment)


def swapped(value, *axes):
    count = 2 ** len(axes)
    name = axes if len(axes) > 1 else axes[0]
    return lax.ppermute(value, name, [(i, i ^ (count - 1)) for i in range(count)])


def both(sent):
    return lax.all_gather(sent, "x", axis=0, tiled=False)


def gathered(block):
    return lax.all_gather(block.astype(jnp.float16), "z", axis=0, tiled=False)


def body(
    tokens_in, section_proj, section_gain, final_gain, score_weight, labels, loss_mask, segment_ids
):
    section = lax.axis_index("s")
    gain_away = swapped(section_gain, "s")

    pieces, gain_away = lax.optimization_barrier((split(section_proj[0]), gain_away))
    half = lax.all_to_all(pieces, ("s", "x"), 0, 0, tiled=True)

    same = gathered(pack(tokens_in, section_gain, gain_away))
    same, half = lax.optimization_barrier((same, half))
    halves = half, swapped(half, "c")
    own, send = product(0, same.astype(BF16), halves)
    first, block = middle(own, both(send), tokens_in, section_gain, gain_away)

    own, send = product(1, gathered(block).astype(BF16), halves)
    second, handed, stats = last(
        own, both(send), first, final_gain[None], score_weight[None]
    )
    handed = swapped(handed, "s")

    stats = lax.all_to_all(stats, ("x", "z"), 0, 0, tiled=True)
    parts = loss_parts(stats, labels, loss_mask, segment_ids)
    parts = lax.all_to_all(parts, ("s", "y", "c"), 0, 0, tiled=True)
    parts = jnp.sum(parts.reshape(2, 8, 2, 128), axis=1)[:, :, :SEGS]
    segment_loss = parts[:, 0] / jnp.maximum(parts[:, 1], 1.0)

    section_out = jnp.where(section == 0, jnp.stack([first, handed]), jnp.stack([handed, second]))
    return section_out[None], segment_loss


def solution(mesh):
    finer = Mesh(mesh.devices.reshape(2, 4, 2, 2, 16), ("s", "y", "c", "x", "z"))
    tensor = ("x", "z")
    dp = ("y", "c")
    in_specs = (
        P(None, tensor, dp),
        P("s", tensor, None),
        P("s", tensor),
        P(tensor),
        P(tensor),
        P(None, dp),
        P(None, dp),
        P(None, dp),
    )
    out_specs = (P("s", None, tensor, dp), P())
    return jax.shard_map(body, mesh=finer, in_specs=in_specs, out_specs=out_specs, check_vma=False)
```

```python
import functools

import jax
import jax.numpy as jnp
from jax import lax
from jax.experimental import pallas as pl
from jax.experimental.pallas import tpu as pltpu
from jax.sharding import Mesh
from jax.sharding import PartitionSpec as P

D = 7168
SEGS = 16
EPS = 1e-05
F = 224
T = 256
KH = D // 2
HALF = F // 2
R = 232
F32 = jnp.float32
BF16 = jnp.bfloat16
SCALE = 32.0
SMALL = pltpu.CompilerParams(vmem_limit_bytes=4 * 1024 * 1024)
WHOLE = pltpu.CompilerParams(vmem_limit_bytes=60 * 1024 * 1024)
LARGE = pltpu.CompilerParams(vmem_limit_bytes=12 * 1024 * 1024)


def vmem():
    return pl.BlockSpec(memory_space=pltpu.VMEM)


def anywhere():
    return pl.BlockSpec(memory_space=pl.ANY)


def column(row):
    down = lax.broadcasted_iota(jnp.int32, (F, F), 0)
    along = lax.broadcasted_iota(jnp.int32, (F, F), 1)
    wide = jnp.where(down == along, jnp.broadcast_to(row.astype(F32), (F, F)), 0.0)
    return jnp.sum(wide, axis=1, keepdims=True)


def picked(here_ref, away_ref, local):
    return column(jnp.where(local, here_ref[...].astype(F32), away_ref[...].astype(F32)))


def pack_block(rows, gain, block_ref):
    block_ref[0:F, :] = ((rows * gain).astype(BF16).astype(F32) * SCALE).astype(BF16)
    block_ref[F:R, :] = three_terms(jnp.sqrt(jnp.sum(rows * rows, axis=0, keepdims=True)))


def call(kernel, outs, ins, out_specs, params, name, scratch=()):
    return pl.pallas_call(
        kernel,
        out_shape=outs,
        in_specs=ins,
        out_specs=out_specs,
        scratch_shapes=scratch,
        compiler_params=params,
        name=name,
    )


def shape(dims, dtype):
    return jax.ShapeDtypeStruct(dims, dtype)


def pack_kernel(tokens_ref, here_ref, away_ref, block_ref):
    section = lax.axis_index("s")
    gain = picked(here_ref, away_ref, section == 0)
    pack_block(tokens_ref[section].astype(F32), gain, block_ref)


def pack(tokens, here, away):
    return call(
        pack_kernel, shape((R, T), BF16), [vmem()] * 3, vmem(), SMALL, "pack"
    )(tokens, here, away)


def split_kernel(weight_ref, out_ref, held, sems):
    rows = pl.ds(pl.multiple_of(lax.axis_index("c") * HALF, 16), HALF)
    loads = []
    for i in range(2):
        columns = pl.ds(i * KH, KH)
        loads.append(
            pltpu.make_async_copy(weight_ref.at[rows, columns], held.at[i], sems.at[4 + i])
        )
    stores = [pltpu.make_async_copy(held.at[i % 2], out_ref.at[i], sems.at[i]) for i in range(4)]
    for load in loads:
        load.start()
    for i in range(2):
        loads[i].wait()
        stores[i].start()
        stores[i + 2].start()
    for store in stores:
        store.wait()


def split(weight):
    return call(
        split_kernel, shape((4, HALF, KH), BF16), [anywhere()], anywhere(), WHOLE, "split",
        [pltpu.VMEM((2, HALF, KH), BF16), pltpu.SemaphoreType.DMA((6,))],
    )(weight)


def three_terms(row):
    first = row.astype(BF16)
    rest = row - first.astype(F32)
    second = rest.astype(BF16)
    third = (rest - second.astype(F32)).astype(BF16)
    at = lax.broadcasted_iota(jnp.int32, (R - F, T), 0)
    tail = jnp.where(at == 0, first.astype(F32), 0.0)
    tail = jnp.where(at == 1, second.astype(F32), tail)
    tail = jnp.where(at == 2, third.astype(F32), tail)
    return tail.astype(BF16)


def product_kernel(
    block, same_ref, terms_ref, half_ref, half2_ref, own_ref, send_ref, held, values, sems
):
    core = lax.axis_index("c")
    x = lax.axis_index("x")
    copies = []
    for i in range(4):
        ref, half = (half_ref, core) if i % 2 == 0 else (half2_ref, 1 - core)
        index, start = (2 * block + x, 0) if i < 2 else (2 * block + 1 - x, F)
        rows = pl.ds(pl.multiple_of(start + half * HALF, 16), HALF)
        copies.append(pltpu.make_async_copy(ref.at[index], held.at[rows, :], sems.at[i]))
    for copy in copies:
        copy.start()

    squares = jnp.zeros((1, T), F32)
    for i in range(16):
        got = same_ref[i]
        values[i * F:(i + 1) * F, :] = got[0:F]
        terms = terms_ref[...] if i == 0 else got[F:R]
        root = jnp.sum(terms.astype(F32), axis=0, keepdims=True)
        squares += root * root

    for copy in copies:
        copy.wait()

    product = jnp.dot(held[...], values[...], preferred_element_type=F32)
    own_ref[0:F, :] = product[0:F]
    own_ref[F:F + 8, :] = jnp.broadcast_to(squares, (8, T))
    send_ref[0:F, :] = product[F:2 * F].astype(BF16)
    send_ref[F:R, :] = three_terms(squares)


def product(block, same, terms, halves):
    return call(
        functools.partial(product_kernel, block),
        (shape((F + 8, T), F32), shape((R, T), BF16)),
        [vmem(), vmem(), anywhere(), anywhere()],
        (vmem(), vmem()),
        LARGE,
        "product",
        [
            pltpu.VMEM((2 * F, KH), BF16),
            pltpu.VMEM((KH, T), BF16),
            pltpu.SemaphoreType.DMA((4,)),
        ],
    )(same.astype(BF16), terms.astype(BF16), *halves)


def block_rows(own_ref, pair_ref, rows):
    sent = pair_ref[1 - lax.axis_index("x")].astype(F32)
    other = jnp.sum(sent[F:R], axis=0, keepdims=True)
    inv_root = lax.rsqrt((own_ref[F:F + 1, :] + other) / D + EPS) / SCALE
    mixed = (own_ref[0:F, :] + sent[0:F]) * inv_root
    gated = mixed / (1.0 + jnp.exp(-mixed))
    return (rows.astype(F32) + gated).astype(BF16)


def middle_kernel(own_ref, pair_ref, tokens_ref, here_ref, away_ref, out_ref, block_ref):
    section = lax.axis_index("s")
    out = block_rows(own_ref, pair_ref, tokens_ref[section])
    out_ref[...] = out
    gain = picked(here_ref, away_ref, section == 1)
    pack_block(out.astype(F32), gain, block_ref)


def middle(own, pair, tokens, here, away):
    return call(
        middle_kernel,
        (shape((F, T), BF16), shape((R, T), BF16)),
        [vmem()] * 5,
        (vmem(), vmem()),
        SMALL,
        "middle",
    )(own, pair, tokens, here, away)


def last_kernel(
    own_ref, pair_ref, rows_ref, gain_ref, score_ref, out_ref, swap_ref, stats_ref
):
    out = block_rows(own_ref, pair_ref, rows_ref[...])
    out_ref[...] = out
    section = lax.axis_index("s")

    @pl.when(section == 0)
    def _():
        swap_ref[...] = out

    @pl.when(section != 0)
    def _():
        swap_ref[...] = rows_ref[...]

    as_float = out.astype(F32)
    head = column(gain_ref[...].astype(F32) * score_ref[...].astype(F32))
    squares = jnp.sum(as_float * as_float, axis=0, keepdims=True)
    scores = jnp.sum(as_float * head, axis=0, keepdims=True)
    stats = jnp.concatenate([squares, scores], axis=0)
    for i in range(32):
        stats_ref[i] = stats


def last(own, pair, rows, gain, score):
    out = shape((F, T), BF16)
    return call(
        last_kernel,
        (out, out, shape((32, 2, T), F32)),
        [vmem()] * 5,
        (vmem(), vmem(), vmem()),
        SMALL,
        "last",
    )(own, pair, rows, gain, score)


def loss_kernel(stats_ref, label_ref, mask_ref, segment_ref, sums_ref):
    first = lax.axis_index("s") == 0

    def pick(ref):
        return jnp.where(first, ref[0:1, :], ref[1:2, :])

    total = jnp.sum(stats_ref[...], axis=0)
    inv_root = lax.rsqrt(total[0:1] / D + EPS)
    score = total[1:2] * inv_root
    target = pick(label_ref).astype(F32) - 1.0
    mask = pick(mask_ref).astype(F32)
    err = score - target
    squared = mask * err * err
    member = pick(segment_ref) == lax.broadcasted_iota(jnp.int32, (SEGS, T), 0)
    sums = jnp.sum(jnp.where(member, squared, 0.0), axis=1, keepdims=True)
    counts = jnp.sum(jnp.where(member, mask, 0.0), axis=1, keepdims=True)
    lane = lax.broadcasted_iota(jnp.int32, (SEGS, 128), 1)
    diagonal = lane == lax.broadcasted_iota(jnp.int32, (SEGS, 128), 0)
    sums = jnp.sum(jnp.where(diagonal, sums, 0.0), axis=0, keepdims=True)
    counts = jnp.sum(jnp.where(diagonal, counts, 0.0), axis=0, keepdims=True)
    both = jnp.concatenate([sums, counts], axis=0)
    for i in range(16):
        sums_ref[i] = both


def loss_parts(stats, label, mask, segment):
    return call(
        loss_kernel, shape((16, 2, 128), F32), [vmem()] * 4, vmem(), SMALL, "loss_parts"
    )(stats, label, mask, segment)


def swapped(value, *axes):
    count = 2 ** len(axes)
    name = axes if len(axes) > 1 else axes[0]
    return lax.ppermute(value, name, [(i, i ^ (count - 1)) for i in range(count)])


def both(sent):
    return lax.all_gather(sent, "x", axis=0, tiled=False)


def gathered(block):
    return lax.all_gather(block.astype(jnp.float16), "z", axis=0, tiled=False)


def body(
    tokens_in, section_proj, section_gain, final_gain, score_weight, labels, loss_mask, segment_ids
):
    section = lax.axis_index("s")
    gain_away = swapped(section_gain, "s")

    pieces, gain_away = lax.optimization_barrier((split(section_proj[0]), gain_away))
    half = lax.all_to_all(pieces, ("s", "x"), 0, 0, tiled=True)

    same = gathered(pack(tokens_in, section_gain, gain_away))
    terms, half = lax.optimization_barrier((same[0, F:R], half))
    halves = half, swapped(half, "c")
    own, send = product(0, same, terms, halves)
    first, block = middle(own, both(send), tokens_in, section_gain, gain_away)

    same = gathered(block)
    own, send = product(1, same, same[0, F:R], halves)
    second, handed, stats = last(
        own, both(send), first, final_gain[None], score_weight[None]
    )
    handed = swapped(handed, "s")

    stats = lax.all_to_all(stats, ("x", "z"), 0, 0, tiled=True)
    parts = loss_parts(stats, labels, loss_mask, segment_ids)
    parts = lax.all_to_all(parts, ("s", "y", "c"), 0, 0, tiled=True)
    parts = jnp.sum(parts.reshape(2, 8, 2, 128), axis=1)[:, :, :SEGS]
    segment_loss = parts[:, 0] / jnp.maximum(parts[:, 1], 1.0)

    section_out = jnp.where(section == 0, jnp.stack([first, handed]), jnp.stack([handed, second]))
    return section_out[None], segment_loss


def solution(mesh):
    finer = Mesh(mesh.devices.reshape(2, 4, 2, 2, 16), ("s", "y", "c", "x", "z"))
    tensor = ("x", "z")
    dp = ("y", "c")
    in_specs = (
        P(None, tensor, dp),
        P("s", tensor, None),
        P("s", tensor),
        P(tensor),
        P(tensor),
        P(None, dp),
        P(None, dp),
        P(None, dp),
    )
    out_specs = (P("s", None, tensor, dp), P())
    return jax.shard_map(body, mesh=finer, in_specs=in_specs, out_specs=out_specs, check_vma=False)
```

```python
import jax
import jax.numpy as jnp
from jax import lax
from jax.experimental import pallas as pl
from jax.experimental.pallas import tpu as pltpu
from jax.sharding import Mesh
from jax.sharding import PartitionSpec as P

D = 7168
SEGS = 16
EPS = 1e-05
F = 224
T = 256
KH = D // 2
HALF = F // 2
R = 232
F32 = jnp.float32
BF16 = jnp.bfloat16
SCALE = 32.0
SMALL = pltpu.CompilerParams(vmem_limit_bytes=4 * 1024 * 1024)
WHOLE = pltpu.CompilerParams(vmem_limit_bytes=60 * 1024 * 1024)
LARGE = pltpu.CompilerParams(vmem_limit_bytes=12 * 1024 * 1024)


def vmem():
    return pl.BlockSpec(memory_space=pltpu.VMEM)


def anywhere():
    return pl.BlockSpec(memory_space=pl.ANY)


def column(row):
    down = lax.broadcasted_iota(jnp.int32, (F, F), 0)
    along = lax.broadcasted_iota(jnp.int32, (F, F), 1)
    wide = jnp.where(down == along, jnp.broadcast_to(row.astype(F32), (F, F)), 0.0)
    return jnp.sum(wide, axis=1, keepdims=True)


def picked(here_ref, away_ref, local):
    return column(jnp.where(local, here_ref[...].astype(F32), away_ref[...].astype(F32)))


def pack_block(rows, gain, block_ref):
    block_ref[0:F, :] = ((rows * gain).astype(BF16).astype(F32) * SCALE).astype(BF16)
    block_ref[F:R, :] = three_terms(jnp.sqrt(jnp.sum(rows * rows, axis=0, keepdims=True)))


def call(kernel, outs, ins, out_specs, params, name, scratch=()):
    return pl.pallas_call(
        kernel,
        out_shape=outs,
        in_specs=ins,
        out_specs=out_specs,
        scratch_shapes=scratch,
        compiler_params=params,
        name=name,
    )


def shape(dims, dtype):
    return jax.ShapeDtypeStruct(dims, dtype)


def pack_kernel(tokens_ref, here_ref, away_ref, block_ref):
    section = lax.axis_index("s")
    gain = picked(here_ref, away_ref, section == 0)
    pack_block(tokens_ref[section].astype(F32), gain, block_ref)


def pack(tokens, here, away):
    return call(
        pack_kernel, shape((R, T), BF16), [vmem()] * 3, vmem(), SMALL, "pack"
    )(tokens, here, away)


def split_kernel(weight_ref, out_ref, held, sems):
    rows = pl.ds(pl.multiple_of(lax.axis_index("c") * HALF, 16), HALF)
    loads = []
    for i in range(2):
        columns = pl.ds(i * KH, KH)
        loads.append(
            pltpu.make_async_copy(weight_ref.at[rows, columns], held.at[i], sems.at[4 + i])
        )
    stores = [pltpu.make_async_copy(held.at[i % 2], out_ref.at[i], sems.at[i]) for i in range(4)]
    for load in loads:
        load.start()
    for i in range(2):
        loads[i].wait()
        stores[i].start()
        stores[i + 2].start()
    for store in stores:
        store.wait()


def split(weight):
    return call(
        split_kernel, shape((4, HALF, KH), BF16), [anywhere()], anywhere(), WHOLE, "split",
        [pltpu.VMEM((2, HALF, KH), BF16), pltpu.SemaphoreType.DMA((6,))],
    )(weight)


def three_terms(row):
    first = row.astype(BF16)
    rest = row - first.astype(F32)
    second = rest.astype(BF16)
    third = (rest - second.astype(F32)).astype(BF16)
    at = lax.broadcasted_iota(jnp.int32, (R - F, T), 0)
    tail = jnp.where(at == 0, first.astype(F32), 0.0)
    tail = jnp.where(at == 1, second.astype(F32), tail)
    tail = jnp.where(at == 2, third.astype(F32), tail)
    return tail.astype(BF16)


def product_kernel(
    same_ref, terms_ref, half_ref, half2_ref, own_ref, send_ref, held, values, sems
):
    core = lax.axis_index("c")
    x = lax.axis_index("x")
    copies = []
    for i in range(4):
        ref, half = (half_ref, core) if i % 2 == 0 else (half2_ref, 1 - core)
        index, start = (x, 0) if i < 2 else (1 - x, F)
        rows = pl.ds(pl.multiple_of(start + half * HALF, 16), HALF)
        copies.append(pltpu.make_async_copy(ref.at[index], held.at[rows, :], sems.at[i]))
    for copy in copies:
        copy.start()

    squares = jnp.zeros((1, T), F32)
    for i in range(16):
        got = same_ref[i]
        values[i * F:(i + 1) * F, :] = got[0:F]
        terms = terms_ref[...] if i == 0 else got[F:R]
        root = jnp.sum(terms.astype(F32), axis=0, keepdims=True)
        squares += root * root

    for copy in copies:
        copy.wait()

    product = jnp.dot(held[...], values[...], preferred_element_type=F32)
    own_ref[0:F, :] = product[0:F]
    own_ref[F:F + 8, :] = jnp.broadcast_to(squares, (8, T))
    send_ref[0:F, :] = product[F:2 * F].astype(BF16)
    send_ref[F:R, :] = three_terms(squares)


def parted_kernel(both_ref, first_ref, second_ref, sems):
    copies = [
        pltpu.make_async_copy(both_ref.at[0:2], first_ref, sems.at[0]),
        pltpu.make_async_copy(both_ref.at[2:4], second_ref, sems.at[1]),
    ]
    for copy in copies:
        copy.start()
    for copy in copies:
        copy.wait()


def parted(both):
    out = shape((2, HALF, KH), BF16)
    return call(
        parted_kernel, (out, out), [anywhere()], (vmem(), vmem()), SMALL, "parted",
        [pltpu.SemaphoreType.DMA((2,))],
    )(both)


def product(same, terms, halves):
    return call(
        product_kernel,
        (shape((F + 8, T), F32), shape((R, T), BF16)),
        [vmem(), vmem(), anywhere(), anywhere()],
        (vmem(), vmem()),
        LARGE,
        "product",
        [
            pltpu.VMEM((2 * F, KH), BF16),
            pltpu.VMEM((KH, T), BF16),
            pltpu.SemaphoreType.DMA((4,)),
        ],
    )(same.astype(BF16), terms.astype(BF16), *halves)


def block_rows(own_ref, pair_ref, rows):
    sent = pair_ref[1 - lax.axis_index("x")].astype(F32)
    other = jnp.sum(sent[F:R], axis=0, keepdims=True)
    inv_root = lax.rsqrt((own_ref[F:F + 1, :] + other) / D + EPS) / SCALE
    mixed = (own_ref[0:F, :] + sent[0:F]) * inv_root
    gated = mixed / (1.0 + jnp.exp(-mixed))
    return (rows.astype(F32) + gated).astype(BF16)


def middle_kernel(own_ref, pair_ref, tokens_ref, here_ref, away_ref, out_ref, block_ref):
    section = lax.axis_index("s")
    out = block_rows(own_ref, pair_ref, tokens_ref[section])
    out_ref[...] = out
    gain = picked(here_ref, away_ref, section == 1)
    pack_block(out.astype(F32), gain, block_ref)


def middle(own, pair, tokens, here, away):
    return call(
        middle_kernel,
        (shape((F, T), BF16), shape((R, T), BF16)),
        [vmem()] * 5,
        (vmem(), vmem()),
        SMALL,
        "middle",
    )(own, pair, tokens, here, away)


def last_kernel(
    own_ref, pair_ref, rows_ref, gain_ref, score_ref, out_ref, swap_ref, stats_ref
):
    out = block_rows(own_ref, pair_ref, rows_ref[...])
    out_ref[...] = out
    section = lax.axis_index("s")

    @pl.when(section == 0)
    def _():
        swap_ref[...] = out

    @pl.when(section != 0)
    def _():
        swap_ref[...] = rows_ref[...]

    as_float = out.astype(F32)
    head = column(gain_ref[...].astype(F32) * score_ref[...].astype(F32))
    squares = jnp.sum(as_float * as_float, axis=0, keepdims=True)
    scores = jnp.sum(as_float * head, axis=0, keepdims=True)
    stats = jnp.concatenate([squares, scores], axis=0)
    for i in range(32):
        stats_ref[i] = stats


def last(own, pair, rows, gain, score):
    out = shape((F, T), BF16)
    return call(
        last_kernel,
        (out, out, shape((32, 2, T), F32)),
        [vmem()] * 5,
        (vmem(), vmem(), vmem()),
        SMALL,
        "last",
    )(own, pair, rows, gain, score)


def loss_kernel(stats_ref, label_ref, mask_ref, segment_ref, sums_ref):
    first = lax.axis_index("s") == 0

    def pick(ref):
        return jnp.where(first, ref[0:1, :], ref[1:2, :])

    total = jnp.sum(stats_ref[...], axis=0)
    inv_root = lax.rsqrt(total[0:1] / D + EPS)
    score = total[1:2] * inv_root
    target = pick(label_ref).astype(F32) - 1.0
    mask = pick(mask_ref).astype(F32)
    err = score - target
    squared = mask * err * err
    member = pick(segment_ref) == lax.broadcasted_iota(jnp.int32, (SEGS, T), 0)
    sums = jnp.sum(jnp.where(member, squared, 0.0), axis=1, keepdims=True)
    counts = jnp.sum(jnp.where(member, mask, 0.0), axis=1, keepdims=True)
    lane = lax.broadcasted_iota(jnp.int32, (SEGS, 128), 1)
    diagonal = lane == lax.broadcasted_iota(jnp.int32, (SEGS, 128), 0)
    sums = jnp.sum(jnp.where(diagonal, sums, 0.0), axis=0, keepdims=True)
    counts = jnp.sum(jnp.where(diagonal, counts, 0.0), axis=0, keepdims=True)
    both = jnp.concatenate([sums, counts], axis=0)
    for i in range(16):
        sums_ref[i] = both


def loss_parts(stats, label, mask, segment):
    return call(
        loss_kernel, shape((16, 2, 128), F32), [vmem()] * 4, vmem(), SMALL, "loss_parts"
    )(stats, label, mask, segment)


def swapped(value, *axes):
    count = 2 ** len(axes)
    name = axes if len(axes) > 1 else axes[0]
    return lax.ppermute(value, name, [(i, i ^ (count - 1)) for i in range(count)])


def both(sent):
    return lax.all_gather(sent, "x", axis=0, tiled=False)


def gathered(block):
    return lax.all_gather(block.astype(jnp.float16), "z", axis=0, tiled=False)


def body(
    tokens_in, section_proj, section_gain, final_gain, score_weight, labels, loss_mask, segment_ids
):
    section = lax.axis_index("s")
    gain_away = swapped(section_gain, "s")

    pieces, gain_away = lax.optimization_barrier((split(section_proj[0]), gain_away))
    half = lax.all_to_all(pieces, ("s", "x"), 0, 0, tiled=True)

    same = gathered(pack(tokens_in, section_gain, gain_away))
    terms, half = lax.optimization_barrier((same[0, F:R], half))
    near, away = parted(half)
    near2, away2 = swapped(near, "c"), swapped(away, "c")
    own, send = product(same, terms, (near, near2))
    first, block = middle(own, both(send), tokens_in, section_gain, gain_away)

    same = gathered(block)
    own, send = product(same, same[0, F:R], (away, away2))
    second, handed, stats = last(
        own, both(send), first, final_gain[None], score_weight[None]
    )
    handed = swapped(handed, "s")

    stats = lax.all_to_all(stats, ("x", "z"), 0, 0, tiled=True)
    parts = loss_parts(stats, labels, loss_mask, segment_ids)
    parts = lax.all_to_all(parts, ("s", "y", "c"), 0, 0, tiled=True)
    parts = jnp.sum(parts.reshape(2, 8, 2, 128), axis=1)[:, :, :SEGS]
    segment_loss = parts[:, 0] / jnp.maximum(parts[:, 1], 1.0)

    section_out = jnp.where(section == 0, jnp.stack([first, handed]), jnp.stack([handed, second]))
    return section_out[None], segment_loss


def solution(mesh):
    finer = Mesh(mesh.devices.reshape(2, 4, 2, 2, 16), ("s", "y", "c", "x", "z"))
    tensor = ("x", "z")
    dp = ("y", "c")
    in_specs = (
        P(None, tensor, dp),
        P("s", tensor, None),
        P("s", tensor),
        P(tensor),
        P(tensor),
        P(None, dp),
        P(None, dp),
        P(None, dp),
    )
    out_specs = (P("s", None, tensor, dp), P())
    return jax.shard_map(body, mesh=finer, in_specs=in_specs, out_specs=out_specs, check_vma=False)
```
